32 devices in a mesh: shot: 2 (over y), row: 4 (over x, core), freq: 4 (over z).
Axes of the slice: x: 2, y: 2, z: 4, core: 2. Of those that a mesh axis runs over, the one named last changes fastest.
Arguments:
- source_field: float32 [2, 8, 1024, 1024], P(None, ('shot', 'freq'), 'row'), parts along dimension 1, may hold values from -6 to 6
- receiver_field: float32 [2, 8, 1024, 1024], P(None, ('shot', 'freq'), 'row'), parts along dimension 1, may hold values from -6 to 6
- slowness: float32 [4, 1024, 1024], P('freq', 'row'), may hold values from 0.22 to 0.67
- owner: int32 [4], replicated, may hold values from 0 to 3, each once
- freq_index: int32 [8], P(('shot', 'freq')), parts along dimension 0, may hold values from 0 to 3, each once
Outputs:
- source_out: float32 [2, 8, 1024, 1024], P(None, ('shot', 'freq'), 'row'), parts along dimension 1
- receiver_out: float32 [2, 8, 1024, 1024], P(None, ('shot', 'freq'), 'row'), parts along dimension 1
- image: float32 [4, 1024, 1024], P('shot', 'row', 'freq'), parts along dimension 0
The draws below stay inside these ranges and needn't reach their ends.
There are 2 independent parts, one for each index of `shot`. The reference program is written for one: setup_inputs(seed, part) draws one part's arguments, and reference() takes and returns one part's arrays. A program takes and returns all parts, laid end to end along the dimension named above; an argument that names none is the same for every part. Nothing has to cross between parts.
All inputs are finite; a program needn't handle non-finite values.
Results may differ from the reference program's by a relative error of at most 0.00022.
Values sent between devices are 32-bit elements; how exact they have to be, the bound alone decides.
A program may use at most 128 MiB of HBM per device.

```python
import math
import jax
import jax.numpy as jnp
from jax import lax

NX = 1024
NY = 1024
NZ = 2
FREQS = 4
SLABS = 4


def level_of(own_key, dims, split, least, top_value):
    level, own = 1.0, jax.random.fold_in(own_key, 6)
    for position, blocks in split:
        heights = jnp.exp(jax.random.uniform(jax.random.fold_in(own, position), (blocks,), jnp.float32, least / len(split), top_value / len(split)))
        level = level * jnp.repeat(heights, dims[position] // blocks).reshape([-1 if axis == position else 1 for axis in range(len(dims))])
    return level


def centred(own_key, extent, scale, reach, split=(), kind=jnp.bfloat16):
    drawn = jax.random.normal(own_key, extent, jnp.float32) * scale
    if len(split) > 0:
        drawn = level_of(own_key, extent, split, -0.22, 0.18) * drawn
    return jnp.clip(drawn, min=-reach, max=reach).astype(kind)


def setup_inputs(seed: int = 0, part: int = 0) -> dict:
    seeds = jax.random.split(jax.random.key(seed), 6)
    part_keys = jax.random.split(jax.random.fold_in(seeds[5], part), 6)
    source_field = centred(part_keys[0], (2, FREQS, NX, NY), 1.0, 6.0, ((1, 4), (2, 4)), jnp.float32)
    receiver_field = centred(part_keys[1], (2, FREQS, NX, NY), 1.0, 6.0, ((1, 4), (2, 4)), jnp.float32)
    slowness = jnp.clip(0.22 + 0.45000002 * jax.random.uniform(seeds[2], (SLABS, NX, NY), jnp.float32) ** level_of(seeds[2], (SLABS, NX, NY), ((0, 4), (1, 4)), -0.2, 0.2), 0.22, 0.67)
    owner = jax.random.permutation(seeds[3], SLABS).astype(jnp.int32)
    freq_index = jax.random.permutation(part_keys[4], FREQS).astype(jnp.int32)
    return dict(source_field=source_field, receiver_field=receiver_field, slowness=slowness, owner=owner, freq_index=freq_index)


dz_km = 0.01
dx_km = 0.0125
ref_slow = 0.5
base_hertz = 3.0
step_hertz = 4.0
taper = 0.5


def wavenumbers(length):
    index = jnp.arange(length, dtype=jnp.int32)
    signed = jnp.where(index * 2 < length, index, index - length)
    return signed.astype(jnp.float32) * (2.0 * math.pi / (length * dx_km))


def reference(source_field, receiver_field, slowness, owner, freq_index):
    kx_all = wavenumbers(NX)
    ky_all = wavenumbers(NY)
    square = kx_all[:, None] ** 2 + ky_all[None, :] ** 2
    kmax = math.pi / dx_km
    damp = jnp.exp(-taper * square / (kmax * kmax))
    omega = 2.0 * math.pi * (base_hertz + step_hertz * freq_index.astype(jnp.float32))
    slabs = [slowness[owner[depth]] for depth in range(NZ)]

    def one_freq(packed):
        omega_one, src_re, src_im, rec_re, rec_im = packed
        source = src_re + 1j * src_im
        receiver = rec_re + 1j * rec_im
        ws0 = omega_one * ref_slow
        vertical = ws0 - 0.5 * square / ws0
        terms = []
        for depth in range(NZ):
            source = jnp.fft.ifft2(jnp.fft.fft2(source) * damp * jnp.exp(1j * dz_km * vertical))
            receiver = jnp.fft.ifft2(jnp.fft.fft2(receiver) * damp * jnp.exp(-1j * dz_km * vertical))
            theta = omega_one * (slabs[depth] - ref_slow) * dz_km
            source = source * jnp.exp(1j * theta)
            receiver = receiver * jnp.exp(-1j * theta)
            terms.append(jnp.real(source) * jnp.real(receiver) + jnp.imag(source) * jnp.imag(receiver))
        return (jnp.real(source), jnp.imag(source), jnp.real(receiver), jnp.imag(receiver), jnp.stack(terms))

    src_re, src_im, rec_re, rec_im, terms = lax.map(
        one_freq, (omega, source_field[0], source_field[1], receiver_field[0], receiver_field[1]))
    image = jnp.sum(terms, axis=0)
    return jnp.stack([src_re, src_im]), jnp.stack([rec_re, rec_im]), image
```

```python
import math
from functools import partial

import jax
import jax.numpy as jnp
import ml_dtypes
import numpy as np
from jax import lax
from jax.experimental import pallas as pl
from jax.experimental.pallas import tpu as pltpu
from jax.sharding import PartitionSpec as P

dz_km = 0.01
dx_km = 0.0125
base_hertz = 3.0
step_hertz = 4.0
taper = 0.5
vmem_bytes = 56 * 1024 * 1024


def split_high_low(value):
    high = lax.reduce_precision(value, 8, 7)
    return high.astype(jnp.bfloat16), (value - high).astype(jnp.bfloat16)


def toeplitz_blocks(length, omega):
    quarter = length // 4
    place = jnp.arange(quarter, dtype=jnp.int32)
    kept = 4 * place[None, :] + jnp.arange(4, dtype=jnp.int32)[:, None]
    signed = jnp.where(kept * 2 < length, kept, kept - length)
    square = (signed.astype(jnp.float32) * (2.0 * math.pi / (length * dx_km))) ** 2
    kmax = math.pi / dx_km
    damp = jnp.exp(-taper * square / (kmax * kmax)) / float(length)
    phase = (-dz_km / omega) * square
    amp_r = (damp * jnp.cos(phase))[:, None, :]
    amp_i = (damp * jnp.sin(phase))[:, None, :]
    turns = (kept[:, None, :] * place[None, :, None] % length).astype(jnp.float32)
    turns = turns * (2.0 * math.pi / length)
    cos_v = jnp.cos(turns)
    sin_v = jnp.sin(turns)
    left = jnp.concatenate([cos_v * amp_r - sin_v * amp_i, sin_v * amp_r + cos_v * amp_i], axis=2)
    right = jnp.concatenate(
        [jnp.concatenate([cos_v, sin_v], axis=2), jnp.concatenate([-sin_v, cos_v], axis=2)], axis=1
    )
    both = jnp.einsum("kbm,kcm->kbc", left, right, precision=lax.Precision.HIGHEST)
    return both[:, :, :quarter], both[:, :, quarter:]


def pack(real, imag, sign):
    top = jnp.concatenate([real, -sign * imag], axis=2)
    low = jnp.concatenate([sign * imag, real], axis=2)
    return split_high_low(jnp.concatenate([top, low], axis=1))


def column_matrix(real, imag):
    return pack(real, imag, 1.0)


def row_matrix(real, imag):
    turned_r = jnp.stack([real[0], real[3], real[2], real[1]])
    turned_i = jnp.stack([imag[0], imag[3], imag[2], imag[1]])
    return pack(turned_r, turned_i, -1.0)


def butterfly(re, im, sign):
    sum_r, dif_r = re[0] + re[2], re[0] - re[2]
    sum_i, dif_i = im[0] + im[2], im[0] - im[2]
    odd_r, gap_r = re[1] + re[3], re[1] - re[3]
    odd_i, gap_i = im[1] + im[3], im[1] - im[3]
    if sign < 0:
        gap_r, gap_i = -gap_r, -gap_i
    out_r = [sum_r + odd_r, dif_r - gap_i, sum_r - odd_r, dif_r + gap_i]
    out_i = [sum_i + odd_i, dif_i + gap_r, sum_i - odd_i, dif_i - gap_r]
    return out_r, out_i


def halves(value):
    high = value.astype(jnp.bfloat16)
    return high, (value - high.astype(jnp.float32)).astype(jnp.bfloat16)


def dot(left, right):
    return jnp.dot(left, right, preferred_element_type=jnp.float32)


def filter_rows(re, im, high_ref, low_ref):
    quarter = re[0].shape[1]
    re, im = butterfly(re, im, -1)
    out_r, out_i = [], []
    for k in range(4):
        high, low = halves(jnp.concatenate([re[k], im[k]], axis=1))
        out = dot(high, high_ref[k]) + (dot(low, high_ref[k]) + dot(high, low_ref[k]))
        out_r.append(out[:, :quarter])
        out_i.append(out[:, quarter:])
    return butterfly(out_r, out_i, 1)


def filter_cols(re, im, high_ref, low_ref):
    quarter = re[0].shape[0]
    re, im = butterfly(re, im, -1)
    out_r, out_i = [], []
    for k in range(4):
        high, low = halves(jnp.concatenate([re[k], im[k]], axis=0))
        out = dot(high_ref[k], high) + (dot(high_ref[k], low) + dot(low_ref[k], high))
        out_r.append(out[:quarter])
        out_i.append(out[quarter:])
    return butterfly(out_r, out_i, 1)


def first_kernel(sign, field_ref, high_ref, low_ref, out_ref):
    quarter = field_ref.shape[3] // 4
    re, im = [], []
    for j in range(4):
        span = pl.ds(j * quarter, quarter)
        re.append(field_ref[0, 0, :, span])
        im.append(sign * field_ref[1, 0, :, span])
    re, im = filter_rows(re, im, high_ref, low_ref)
    for j in range(4):
        out_ref[j, 0] = re[j]
        out_ref[j, 1] = im[j]


def middle_step(cos_ref, sin_ref, field_ref, high_ref, low_ref, out_ref, keep):
    re = [field_ref[j, 0] for j in range(4)]
    im = [field_ref[j, 1] for j in range(4)]
    re, im = filter_cols(re, im, high_ref, low_ref)
    for j in range(4):
        cos_v, sin_v = cos_ref[j], sin_ref[j]
        re[j], im[j] = re[j] * cos_v - im[j] * sin_v, im[j] * cos_v + re[j] * sin_v
        keep(j, re[j], im[j])
    re, im = filter_cols(re, im, high_ref, low_ref)
    for j in range(4):
        out_ref[j, 0] = re[j]
        out_ref[j, 1] = im[j]


def middle_source(cos_ref, sin_ref, field_ref, high_ref, low_ref, out_ref, mid_ref):
    def keep(j, re, im):
        mid_ref[j, 0] = re
        mid_ref[j, 1] = im

    middle_step(cos_ref, sin_ref, field_ref, high_ref, low_ref, out_ref, keep)


def middle_receiver(cos_ref, sin_ref, field_ref, high_ref, low_ref, mid_ref, out_ref, term_ref):
    def keep(j, re, im):
        term_ref[j] = mid_ref[j, 0] * re - mid_ref[j, 1] * im

    middle_step(cos_ref, sin_ref, field_ref, high_ref, low_ref, out_ref, keep)


def last_step(cos_ref, sin_ref, field_ref, high_ref, low_ref, keep):
    quarter = field_ref.shape[3]
    re = [field_ref[j, 0] for j in range(4)]
    im = [field_ref[j, 1] for j in range(4)]
    re, im = filter_rows(re, im, high_ref, low_ref)
    for j in range(4):
        span = pl.ds(j * quarter, quarter)
        cos_v, sin_v = cos_ref[:, span], sin_ref[:, span]
        keep(span, re[j] * cos_v - im[j] * sin_v, im[j] * cos_v + re[j] * sin_v)


def last_source(cos_ref, sin_ref, field_ref, high_ref, low_ref, source_ref):
    def keep(span, re, im):
        source_ref[0, 0, :, span] = re
        source_ref[1, 0, :, span] = im

    last_step(cos_ref, sin_ref, field_ref, high_ref, low_ref, keep)


def last_receiver(cos_ref, sin_ref, field_ref, high_ref, low_ref, source_ref, receiver_ref, term_ref):
    def keep(span, re, im):
        term_ref[span.start // span.size] = (
            source_ref[0, 0, :, span] * re - source_ref[1, 0, :, span] * im
        )
        receiver_ref[0, 0, :, span] = re
        receiver_ref[1, 0, :, span] = -im

    last_step(cos_ref, sin_ref, field_ref, high_ref, low_ref, keep)


def params():
    return pltpu.CompilerParams(vmem_limit_bytes=vmem_bytes, dimension_semantics=("arbitrary",))


def whole(shape):
    return pl.BlockSpec(shape, lambda i: (0,) * len(shape))


def swap(blocks):
    return lax.all_to_all(blocks, "row", split_axis=0, concat_axis=0, tiled=True)


def sum_strips(strips):
    count = strips.shape[0]
    me = lax.axis_index("freq")
    total = lax.dynamic_index_in_dim(strips, me, 0, keepdims=False)
    for shift in range(1, count):
        sent = lax.dynamic_index_in_dim(strips, (me + shift) % count, 0, keepdims=False)
        total = total + lax.ppermute(sent, "freq", [(i, (i + shift) % count) for i in range(count)])
    return total


def body(source_field, receiver_field, slowness, owner, freq_index):
    rows, width = source_field.shape[2:]
    row_count = lax.axis_size("row")
    freq_count = lax.axis_size("freq")
    height = rows * row_count
    cols = width // row_count
    quart_w = width // 4
    quart_h = height // 4
    more = row_count // 4
    omega = 2.0 * math.pi * (base_hertz + step_hertz * freq_index.astype(jnp.float32))

    def turning(slab):
        theta = slab * (omega[0] * dz_km)
        return jnp.cos(theta), jnp.sin(theta)

    def owned(depth):
        return jnp.where(lax.axis_index("freq") == owner[depth], slowness[0], 0.0)

    turned = swap(jnp.moveaxis(owned(0).reshape(rows, row_count, cols), 1, 0))
    piece_last = lax.psum_scatter(owned(1), "freq", scatter_dimension=0, tiled=True)
    source_field, turned = lax.optimization_barrier((source_field, turned))
    turned, piece_last = lax.optimization_barrier((turned, piece_last))
    piece = lax.psum_scatter(turned, "freq", scatter_dimension=0, tiled=True)
    receiver_field, piece = lax.optimization_barrier((receiver_field, piece))
    slab_first = lax.all_gather(piece, "freq", axis=0, tiled=True)
    piece_last, slab_first = lax.optimization_barrier((piece_last, slab_first))
    slab_last = lax.all_gather(piece_last, "freq", axis=0, tiled=True)
    turn_first = turning(slab_first.reshape(4, quart_h, cols))

    block_w = toeplitz_blocks(width, omega[0])
    block_h = block_w if height == width else toeplitz_blocks(height, omega[0])
    row_high, row_low = row_matrix(*block_w)
    col_high, col_low = column_matrix(*block_h)
    mat_w = whole((4, 2 * quart_w, 2 * quart_w))
    mat_h = whole((4, 2 * quart_h, 2 * quart_h))

    step = min(rows, 128)
    row_block = pl.BlockSpec((2, 1, step, width), lambda i: (0, 0, i, 0))
    quarter_block = pl.BlockSpec((4, 2, step, quart_w), lambda i: (0, 0, i, 0))
    line_block = pl.BlockSpec((step, width), lambda i: (i, 0))
    col_block = pl.BlockSpec((4, 2, quart_h, cols), lambda i: (0, 0, 0, 0))
    term_block = pl.BlockSpec((4, quart_h, cols), lambda i: (0, 0, 0))
    quarter_shape = jax.ShapeDtypeStruct((4, 2, rows, quart_w), jnp.float32)
    col_shape = jax.ShapeDtypeStruct((4, 2, quart_h, cols), jnp.float32)
    term_shape = jax.ShapeDtypeStruct((4, quart_h, cols), jnp.float32)
    strip_block = pl.BlockSpec((4, step, quart_w), lambda i: (0, i, 0))
    strip_shape = jax.ShapeDtypeStruct((4, rows, quart_w), jnp.float32)
    field_shape = jax.ShapeDtypeStruct(source_field.shape, jnp.float32)

    def first(field, sign):
        return pl.pallas_call(
            partial(first_kernel, sign),
            grid=(rows // step,),
            in_specs=[row_block, mat_w, mat_w],
            out_specs=quarter_block,
            out_shape=quarter_shape,
            compiler_params=params(),
        )(field, row_high, row_low)

    def to_cols(fields):
        if more > 1:
            fields = fields.reshape(4, 2, rows, more, cols)
            fields = jnp.moveaxis(fields, 3, 1).reshape(row_count, 2, rows, cols)
        fields = swap(fields)
        if more > 1:
            fields = fields.reshape(4, more, 2, rows, cols)
            fields = jnp.moveaxis(fields, 1, 2).reshape(4, 2, quart_h, cols)
        return fields

    def to_rows(fields):
        if more > 1:
            fields = fields.reshape(4, 2, more, rows, cols)
            fields = jnp.moveaxis(fields, 2, 1).reshape(row_count, 2, rows, cols)
        fields = swap(fields)
        if more > 1:
            fields = fields.reshape(4, more, 2, rows, cols)
            fields = jnp.moveaxis(fields, 1, 3).reshape(4, 2, rows, quart_w)
        return fields

    source = to_cols(first(source_field, 1.0))
    receiver = to_cols(first(receiver_field, -1.0))
    source, middle = pl.pallas_call(
        middle_source,
        grid=(1,),
        in_specs=[term_block, term_block, col_block, mat_h, mat_h],
        out_specs=[col_block, col_block],
        out_shape=[col_shape, col_shape],
        compiler_params=params(),
    )(*turn_first, source, col_high, col_low)
    source = to_rows(source)
    receiver, term = pl.pallas_call(
        middle_receiver,
        grid=(1,),
        in_specs=[term_block, term_block, col_block, mat_h, mat_h, col_block],
        out_specs=[col_block, term_block],
        out_shape=[col_shape, term_shape],
        compiler_params=params(),
    )(*turn_first, receiver, col_high, col_low, middle)
    receiver, term, slab_last = lax.optimization_barrier((receiver, term, slab_last))
    turn_last = turning(slab_last)
    receiver = to_rows(receiver)

    term = term.reshape(height, cols)
    if row_count == freq_count:
        part = lax.psum_scatter(term, "freq", scatter_dimension=0, tiled=True)
        pairs = [
            (r * freq_count + f, f * freq_count + r)
            for r in range(row_count)
            for f in range(freq_count)
        ]
        image_first = lax.ppermute(part, ("row", "freq"), pairs)
    else:
        term = lax.all_to_all(term, "row", split_axis=0, concat_axis=1, tiled=True)
        image_first = lax.psum_scatter(term, "freq", scatter_dimension=1, tiled=True)

    source_out = pl.pallas_call(
        last_source,
        grid=(rows // step,),
        in_specs=[line_block, line_block, quarter_block, mat_w, mat_w],
        out_specs=row_block,
        out_shape=field_shape,
        compiler_params=params(),
    )(*turn_last, source, row_high, row_low)
    receiver_out, term = pl.pallas_call(
        last_receiver,
        grid=(rows // step,),
        in_specs=[line_block, line_block, quarter_block, mat_w, mat_w, row_block],
        out_specs=[row_block, strip_block],
        out_shape=[field_shape, strip_shape],
        compiler_params=params(),
    )(*turn_last, receiver, row_high, row_low, source_out)
    if freq_count == 4:
        image_last = sum_strips(term)
    else:
        term = jnp.moveaxis(term, 0, 1).reshape(rows, width)
        image_last = lax.psum_scatter(term, "freq", scatter_dimension=1, tiled=True)
    return source_out, receiver_out, jnp.stack([image_first, image_last])


fused_vmem = 60 * 1024 * 1024
MESH = pl.DeviceIdType.MESH


def filter_table(length, count):
    quarter = length // 4
    offset = np.arange(1 - quarter, quarter)
    place = np.arange(quarter)
    delta = place[:, None] - place[None, :] + quarter - 1
    table = np.zeros((count, 8, 2 * quarter, 2 * quarter), ml_dtypes.bfloat16)
    kmax = math.pi / dx_km
    for slot in range(count):
        omega = 2.0 * math.pi * (base_hertz + step_hertz * slot)
        for k in range(4):
            kept = 4 * place + k
            signed = np.where(kept * 2 < length, kept, kept - length)
            square = (signed * (2.0 * math.pi / (length * dx_km))) ** 2
            amp = np.exp(-taper * square / kmax**2 - 1j * (dz_km / omega) * square) / length
            turns = (offset[:, None] * kept[None, :]) % length
            kernel = np.exp(2j * math.pi / length * turns) @ amp
            block = kernel[delta]
            full = np.block([[block.real, -block.imag], [block.imag, block.real]]).astype(np.float32)
            high = full.astype(ml_dtypes.bfloat16)
            table[slot, k] = high
            table[slot, 4 + k] = (full - high.astype(np.float32)).astype(ml_dtypes.bfloat16)
    return table


def turn_of(theta):
    square = theta * theta
    cos_v = 1.0 / 87178291200.0
    sin_v = 1.0 / 1307674368000.0
    cos_v = 1.0 / 479001600.0 - square * cos_v
    sin_v = 1.0 / 6227020800.0 - square * sin_v
    for even in (10, 8, 6, 4, 2, 0):
        cos_v = 1.0 / math.factorial(even) - square * cos_v
        sin_v = 1.0 / math.factorial(even + 1) - square * sin_v
    return cos_v, theta * sin_v


def row_pass(re, im, mats):
    step, quarter = re[0].shape
    re, im = butterfly(re, im, 1)
    out_r, out_i = [], []
    for k in range(4):
        turned = (4 - k) % 4
        high, low = halves(jnp.concatenate([re[k], im[k]], axis=1))
        out = dot(jnp.concatenate([high, low], axis=0), mats[turned])
        out = out[:step] + (out[step:] + dot(high, mats[4 + turned]))
        out_r.append(out[:, :quarter])
        out_i.append(out[:, quarter:])
    return butterfly(out_r, out_i, -1)


def col_pass(re, im, mats):
    quarter = re[0].shape[0]
    re, im = butterfly(re, im, -1)
    out_r, out_i = [], []
    for k in range(4):
        high, low = halves(jnp.concatenate([re[k], im[k]], axis=0))
        out = dot(mats[k], high) + (dot(mats[k], low) + dot(mats[4 + k], high))
        out_r.append(out[:quarter])
        out_i.append(out[quarter:])
    return butterfly(out_r, out_i, 1)


def wait_for(ref, sem):
    pltpu.make_async_copy(ref, ref, sem).wait()


def fused_kernel(
    step, scal, src_in, rec_in, slow_in, mat_in, src_out, rec_out, img_out,
    field, mats, slab, early, cols, mid, late, lines, masked, shared, piece, grid_first, grid_last,
    cos_first, sin_first, cos_last, sin_last, term_first, got_first, part_first, term_last, got_last, image,
    load_sem, store_sem, early_send, cols_recv, own_sem, late_send, lines_recv,
    shared_send, shared_recv, piece_send, piece_recv, depth_send, depth_recv, across_send, across_recv,
    first_send, first_recv, cross_send, cross_recv, last_send, last_recv,
):
    shot, row, freq = lax.axis_index("shot"), lax.axis_index("row"), lax.axis_index("freq")
    rows, width = slab.shape
    quarter = width // 4
    chunks = rows // step
    eighth = rows // 8
    chip, core = lax.div(row, 2), lax.rem(row, 2)
    row_peers = [(1 - chip) * 2 + core, (1 - chip) * 2 + 1 - core, chip * 2 + 1 - core]
    freq_peers = [lax.rem(freq + 1, 4), lax.rem(freq + 3, 4), lax.rem(freq + 2, 4)]

    def send(source, target, send_sem, recv_sem, device):
        pltpu.make_async_remote_copy(
            src_ref=source, dst_ref=target, send_sem=send_sem, recv_sem=recv_sem,
            device_id=device, device_id_type=MESH,
        ).start()

    def span(c):
        return pl.ds(pl.multiple_of(c * step, step), step)

    loads = [
        pltpu.make_async_copy(src_in.at[:, 0], field.at[0], load_sem.at[0]),
        pltpu.make_async_copy(mat_in, mats, load_sem.at[1]),
        pltpu.make_async_copy(slow_in.at[0], slab, load_sem.at[2]),
        pltpu.make_async_copy(rec_in.at[:, 0], field.at[1], load_sem.at[3]),
    ]
    for load in loads:
        load.start()

    barrier = pltpu.get_barrier_semaphore()
    peers = [(shot, peer, freq) for peer in row_peers] + [(shot, row, peer) for peer in freq_peers]
    for device in peers + [(1 - shot, row, freq)]:
        pl.semaphore_signal(barrier, inc=1, device_id=device, device_id_type=MESH)

    @pl.when(row != freq)
    def _():
        pl.semaphore_signal(barrier, inc=1, device_id=(shot, freq, row), device_id_type=MESH)
        pl.semaphore_wait(barrier, 8)

    @pl.when(row == freq)
    def _():
        pl.semaphore_wait(barrier, 7)

    def early_rows(which, c):
        place = span(c)
        re = [field[which, 0, place, j * quarter : (j + 1) * quarter] for j in range(4)]
        im = [field[which, 1, place, j * quarter : (j + 1) * quarter] for j in range(4)]
        if which == 0:
            im = [-v for v in im]
        re, im = row_pass(re, im, mats)
        for j in range(4):
            early[which, c, j, 0] = re[j]
            early[which, c, j, 1] = -im[j]

    def early_go(which, c):
        target = cols.at[which, row, :, span(c), :]
        for peer in row_peers:
            send(early.at[which, c, peer], target, early_send.at[which, c], cols_recv.at[which], (shot, peer, freq))
        pltpu.make_async_copy(early.at[which, c, row], target, own_sem.at[0, which]).start()

    def early_sent(which, c):
        wait_for(early.at[which, c, pl.ds(0, 3)], early_send.at[which, c])

    def late_go(which, c):
        target = lines.at[which, row, :, span(c), :]
        for peer in row_peers:
            send(late.at[which, peer, :, span(c), :], target, late_send.at[which, c], lines_recv.at[which, c], (shot, peer, freq))

    def late_sent(which, c):
        wait_for(late.at[which, pl.ds(0, 3), :, span(c), :], late_send.at[which, c])

    def share_go(depth):
        for peer in freq_peers:
            send(masked.at[depth, peer], shared.at[depth, freq], shared_send.at[depth], shared_recv.at[depth], (shot, row, peer))

    def share_sum(depth):
        shared[depth, freq] = masked[depth, freq]
        wait_for(shared.at[depth, pl.ds(0, 3)], shared_recv.at[depth])
        return (shared[depth, 0] + shared[depth, 1]) + (shared[depth, 2] + shared[depth, 3])

    def gather_go(depth, ref):
        for peer in freq_peers:
            send(ref.at[shot, freq], ref.at[shot, freq], depth_send.at[depth], depth_recv.at[depth, freq], (shot, row, peer))
        send(ref.at[shot, freq], ref.at[shot, freq], across_send.at[depth], across_recv.at[depth], (1 - shot, row, freq))

    def gather_end(depth, ref):
        for peer in freq_peers:
            block = ref.at[shot, peer]
            wait_for(block, depth_recv.at[depth, peer])
            send(block, block, across_send.at[depth], across_recv.at[depth], (1 - shot, row, freq))

    def gather_wait(depth, ref):
        wait_for(ref.at[1 - shot], across_recv.at[depth])

    loads[1].wait()
    loads[0].wait()
    early_rows(0, 0)
    early_go(0, 0)
    loads[2].wait()
    for depth in range(2):
        for k in range(4):
            base = pl.multiple_of((shot * 4 + k) * eighth, eighth)
            masked[depth, k] = slab[pl.ds(base, eighth), :] * scal[1 + depth]
    share_go(0)

    @pl.loop(1, chunks)
    def _(c):
        early_rows(0, c)
        early_go(0, c)

    loads[3].wait()

    @pl.loop(0, chunks)
    def _(c):
        early_rows(1, c)

    total = share_sum(0)
    for j in range(4):
        piece[j] = total[:, j * quarter : (j + 1) * quarter]
    for peer in row_peers:
        send(piece.at[peer], grid_first.at[shot, freq, row], piece_send, piece_recv, (shot, peer, freq))
    grid_first[shot, freq, row] = piece[row]
    share_go(1)
    for c in range(chunks - 1):
        early_sent(0, c)
    early_go(1, 0)
    wait_for(grid_first.at[shot, freq, pl.ds(0, 3)], piece_recv)
    gather_go(0, grid_first)
    early_sent(0, chunks - 1)
    early_go(1, 1)

    def col_ready(which):
        wait_for(cols.at[which, 0], own_sem.at[0, which])
        wait_for(cols.at[which, pl.ds(0, 3)], cols_recv.at[which])

    def col_first(which):
        return col_pass([cols[which, j, 0] for j in range(4)], [cols[which, j, 1] for j in range(4)], mats)

    def turned(j, re, im):
        return re * cos_first[j] - im * sin_first[j], im * cos_first[j] + re * sin_first[j]

    def col_second(which, re, im):
        re, im = col_pass(re, im, mats)
        for j in range(4):
            late[which, j, 0] = re[j]
            late[which, j, 1] = im[j]
        pltpu.make_async_copy(late.at[which, row], lines.at[which, row], own_sem.at[1, which]).start()

    col_ready(0)
    re, im = col_first(0)
    for j in range(4):
        mid[j, 0] = re[j]
        mid[j, 1] = im[j]
    early_sent(1, 0)
    early_go(1, 2)
    gather_end(0, grid_first)
    early_sent(1, 1)
    early_go(1, 3)
    gather_wait(0, grid_first)
    for j in range(4):
        theta = grid_first[:, :, j].reshape(rows, quarter) * scal[0]
        cos_first[j], sin_first[j] = turn_of(theta)
    re, im = [], []
    for j in range(4):
        real, imag = turned(j, mid[j, 0], mid[j, 1])
        mid[j, 0] = real
        mid[j, 1] = imag
        re.append(real)
        im.append(imag)
    col_second(0, re, im)
    for c in range(chunks):
        late_go(0, c)
    grid_last[shot, freq] = share_sum(1)
    gather_go(1, grid_last)

    col_ready(1)
    re, im = col_first(1)
    for j in range(4):
        re[j], im[j] = turned(j, re[j], im[j])
        term_first[j] = mid[j, 0] * re[j] - mid[j, 1] * im[j]
    for peer in freq_peers:
        send(term_first.at[peer], got_first.at[freq], first_send, first_recv, (shot, row, peer))
    col_second(1, re, im)

    gather_end(1, grid_last)
    gather_wait(1, grid_last)
    cos_last[...], sin_last[...] = turn_of(grid_last[...].reshape(rows, width) * scal[0])

    def final_rows(which, c):
        place = span(c)
        wait_for(lines.at[which, pl.ds(0, 3), :, place, :], lines_recv.at[which, c])
        re = [lines[which, j, 0, place, :] for j in range(4)]
        im = [-lines[which, j, 1, place, :] for j in range(4)]
        re, im = row_pass(re, im, mats)
        for j in range(4):
            here = slice(j * quarter, (j + 1) * quarter)
            cos_v, sin_v = cos_last[place, here], sin_last[place, here]
            real = re[j] * cos_v + im[j] * sin_v
            imag = im[j] * cos_v - re[j] * sin_v
            if which == 0:
                imag = -imag
            else:
                term_last[c, j] = field[0, 0, place, here] * real + field[0, 1, place, here] * imag
            field[which, 0, place, here] = real
            field[which, 1, place, here] = imag
        out = (src_out, rec_out)[which]
        pltpu.make_async_copy(field.at[which, :, place, :], out.at[:, 0, place, :], store_sem.at[which]).start()

    for c in range(chunks - 1):
        late_sent(0, c)
    late_go(1, 0)
    late_sent(0, chunks - 1)
    late_go(1, 1)
    wait_for(late.at[0, 0], own_sem.at[1, 0])
    wait_for(late.at[1, 0], own_sem.at[1, 1])

    @pl.loop(0, chunks)
    def _(c):
        final_rows(0, c)

    late_sent(1, 0)
    late_go(1, 2)
    got_first[freq] = term_first[freq]
    wait_for(got_first.at[pl.ds(0, 3)], first_recv)
    part_first[...] = (got_first[0] + got_first[1]) + (got_first[2] + got_first[3])

    @pl.when(row != freq)
    def _():
        send(part_first, image.at[0], cross_send, cross_recv, (shot, freq, row))

    @pl.when(row == freq)
    def _():
        image[0] = part_first[...]

    late_sent(1, 1)
    late_go(1, 3)

    @pl.loop(0, chunks)
    def _(c):
        final_rows(1, c)
        for peer in freq_peers:
            send(term_last.at[c, peer], got_last.at[freq, c], last_send, last_recv.at[c], (shot, row, peer))

    got_last[freq] = term_last[:, freq]

    @pl.when(row != freq)
    def _():
        wait_for(image.at[0], cross_recv)
        wait_for(part_first, cross_send)

    pltpu.make_async_copy(image.at[0], img_out.at[0], store_sem.at[2]).start()

    @pl.loop(0, chunks)
    def _(c):
        wait_for(got_last.at[pl.ds(0, 3), c], last_recv.at[c])
        image[1, span(c), :] = (got_last[0, c] + got_last[1, c]) + (got_last[2, c] + got_last[3, c])

    pltpu.make_async_copy(image.at[1], img_out.at[1], store_sem.at[3]).start()

    wait_for(piece.at[pl.ds(0, 3)], piece_send)
    for depth, ref in enumerate((grid_first, grid_last)):
        wait_for(masked.at[depth, pl.ds(0, 3)], shared_send.at[depth])
        wait_for(ref.at[0, pl.ds(0, 3)], depth_send.at[depth])
        wait_for(ref.at[0], across_send.at[depth])
    for c in (2, 3):
        early_sent(1, c)
        late_sent(1, c)
    wait_for(term_first.at[pl.ds(0, 3)], first_send)
    wait_for(term_last.at[:, pl.ds(0, 3)], last_send)
    wait_for(field.at[0], store_sem.at[0])
    wait_for(field.at[1], store_sem.at[1])
    wait_for(image.at[0], store_sem.at[2])
    wait_for(image.at[1], store_sem.at[3])


def fused_body(table, source_field, receiver_field, slowness, owner, freq_index):
    rows, width = source_field.shape[2:]
    quarter = width // 4
    chunks = 4
    step = rows // chunks
    omega = 2.0 * math.pi * (base_hertz + step_hertz * freq_index.astype(jnp.float32))
    mine = (owner[:2] == lax.axis_index("freq")).astype(jnp.float32)
    scal = jnp.concatenate([omega * dz_km, mine, jnp.zeros((1,), jnp.float32)])
    matrix = lax.dynamic_index_in_dim(table, freq_index[0], 0, keepdims=False)

    def floats(*shape):
        return pltpu.VMEM(shape, jnp.float32)

    dma = pltpu.SemaphoreType.DMA
    block = (4, 2, rows, quarter)
    any_spec = pl.BlockSpec(memory_space=pl.ANY)
    return pl.pallas_call(
        partial(fused_kernel, step),
        out_shape=[
            jax.ShapeDtypeStruct(source_field.shape, jnp.float32),
            jax.ShapeDtypeStruct(source_field.shape, jnp.float32),
            jax.ShapeDtypeStruct((2, rows, quarter), jnp.float32),
        ],
        in_specs=[pl.BlockSpec(memory_space=pltpu.SMEM)] + [any_spec] * 4,
        out_specs=[any_spec] * 3,
        scratch_shapes=[
            floats(2, 2, rows, width),
            pltpu.VMEM(matrix.shape, jnp.bfloat16),
            floats(rows, width),
            floats(2, chunks, 4, 2, step, quarter),
            floats(2, *block),
            floats(*block),
            floats(2, *block),
            floats(2, *block),
            floats(2, 4, rows // 8, width),
            floats(2, 4, rows // 8, width),
            floats(4, rows // 8, quarter),
            floats(2, 4, 4, rows // 8, quarter),
            floats(2, 4, rows // 8, width),
            floats(4, rows, quarter),
            floats(4, rows, quarter),
            floats(rows, width),
            floats(rows, width),
            floats(4, rows, quarter),
            floats(4, rows, quarter),
            floats(rows, quarter),
            floats(chunks, 4, step, quarter),
            floats(4, chunks, step, quarter),
            floats(2, rows, quarter),
            dma((4,)), dma((4,)), dma((2, chunks)), dma((2,)), dma((2, 2)), dma((2, chunks)), dma((2, chunks)),
            dma((2,)), dma((2,)), dma, dma, dma((2,)), dma((2, 4)), dma((2,)), dma((2,)),
            dma, dma, dma, dma, dma, dma((chunks,)),
        ],
        compiler_params=pltpu.CompilerParams(
            collective_id=0, has_side_effects=True, vmem_limit_bytes=fused_vmem
        ),
    )(scal, source_field, receiver_field, slowness, matrix)


def solution(mesh):
    in_specs = (
        P(None, ("shot", "freq"), "row", None),
        P(None, ("shot", "freq"), "row", None),
        P("freq", "row", None),
        P(),
        P(("shot", "freq")),
    )
    out_specs = (
        P(None, ("shot", "freq"), "row", None),
        P(None, ("shot", "freq"), "row", None),
        P("shot", "row", "freq"),
    )
    sizes = tuple(mesh.shape[name] for name in ("shot", "row", "freq"))

    def whole_program(source_field, *rest):
        height, width = source_field.shape[2:]
        part = body
        if sizes == (2, 4, 4) and height == width and width % 512 == 0:
            part = partial(fused_body, filter_table(width, sizes[2]))
        return jax.shard_map(part, mesh=mesh, in_specs=in_specs, out_specs=out_specs, check_vma=False)(
            source_field, *rest
        )

    return whole_program
```

```python
import math
from functools import partial

import jax
import jax.numpy as jnp
import numpy as np
from jax import lax
from jax.experimental import pallas as pl
from jax.experimental.pallas import tpu as pltpu
from jax.sharding import PartitionSpec as P

dz_km = 0.01
dx_km = 0.0125
base_hertz = 3.0
step_hertz = 4.0
taper = 0.5
vmem_bytes = 56 * 1024 * 1024


def split_high_low(value):
    high = lax.reduce_precision(value, 8, 7)
    return high.astype(jnp.bfloat16), (value - high).astype(jnp.bfloat16)


def toeplitz_blocks(length, omega):
    quarter = length // 4
    place = jnp.arange(quarter, dtype=jnp.int32)
    kept = 4 * place[None, :] + jnp.arange(4, dtype=jnp.int32)[:, None]
    signed = jnp.where(kept * 2 < length, kept, kept - length)
    square = (signed.astype(jnp.float32) * (2.0 * math.pi / (length * dx_km))) ** 2
    kmax = math.pi / dx_km
    damp = jnp.exp(-taper * square / (kmax * kmax)) / float(length)
    phase = (-dz_km / omega) * square
    amp_r = (damp * jnp.cos(phase))[:, None, :]
    amp_i = (damp * jnp.sin(phase))[:, None, :]
    turns = (kept[:, None, :] * place[None, :, None] % length).astype(jnp.float32)
    turns = turns * (2.0 * math.pi / length)
    cos_v = jnp.cos(turns)
    sin_v = jnp.sin(turns)
    left = jnp.concatenate([cos_v * amp_r - sin_v * amp_i, sin_v * amp_r + cos_v * amp_i], axis=2)
    right = jnp.concatenate(
        [jnp.concatenate([cos_v, sin_v], axis=2), jnp.concatenate([-sin_v, cos_v], axis=2)], axis=1
    )
    both = jnp.einsum("kbm,kcm->kbc", left, right, precision=lax.Precision.HIGHEST)
    return both[:, :, :quarter], both[:, :, quarter:]


def pack(real, imag, sign):
    top = jnp.concatenate([real, -sign * imag], axis=2)
    low = jnp.concatenate([sign * imag, real], axis=2)
    return split_high_low(jnp.concatenate([top, low], axis=1))


def column_matrix(real, imag):
    return pack(real, imag, 1.0)


def row_matrix(real, imag):
    turned_r = jnp.stack([real[0], real[3], real[2], real[1]])
    turned_i = jnp.stack([imag[0], imag[3], imag[2], imag[1]])
    return pack(turned_r, turned_i, -1.0)


def butterfly(re, im, sign):
    sum_r, dif_r = re[0] + re[2], re[0] - re[2]
    sum_i, dif_i = im[0] + im[2], im[0] - im[2]
    odd_r, gap_r = re[1] + re[3], re[1] - re[3]
    odd_i, gap_i = im[1] + im[3], im[1] - im[3]
    if sign < 0:
        gap_r, gap_i = -gap_r, -gap_i
    out_r = [sum_r + odd_r, dif_r - gap_i, sum_r - odd_r, dif_r + gap_i]
    out_i = [sum_i + odd_i, dif_i + gap_r, sum_i - odd_i, dif_i - gap_r]
    return out_r, out_i


def halves(value):
    high = value.astype(jnp.bfloat16)
    return high, (value - high.astype(jnp.float32)).astype(jnp.bfloat16)


def dot(left, right):
    return jnp.dot(left, right, preferred_element_type=jnp.float32)


def filter_rows(re, im, high_ref, low_ref):
    quarter = re[0].shape[1]
    re, im = butterfly(re, im, -1)
    out_r, out_i = [], []
    for k in range(4):
        high, low = halves(jnp.concatenate([re[k], im[k]], axis=1))
        out = dot(high, high_ref[k]) + (dot(low, high_ref[k]) + dot(high, low_ref[k]))
        out_r.append(out[:, :quarter])
        out_i.append(out[:, quarter:])
    return butterfly(out_r, out_i, 1)


def filter_cols(re, im, high_ref, low_ref):
    quarter = re[0].shape[0]
    re, im = butterfly(re, im, -1)
    out_r, out_i = [], []
    for k in range(4):
        high, low = halves(jnp.concatenate([re[k], im[k]], axis=0))
        out = dot(high_ref[k], high) + (dot(high_ref[k], low) + dot(low_ref[k], high))
        out_r.append(out[:quarter])
        out_i.append(out[quarter:])
    return butterfly(out_r, out_i, 1)


def first_kernel(sign, field_ref, high_ref, low_ref, out_ref):
    quarter = field_ref.shape[3] // 4
    re, im = [], []
    for j in range(4):
        span = pl.ds(j * quarter, quarter)
        re.append(field_ref[0, 0, :, span])
        im.append(sign * field_ref[1, 0, :, span])
    re, im = filter_rows(re, im, high_ref, low_ref)
    for j in range(4):
        out_ref[j, 0] = re[j]
        out_ref[j, 1] = im[j]


def middle_step(cos_ref, sin_ref, field_ref, high_ref, low_ref, out_ref, keep):
    re = [field_ref[j, 0] for j in range(4)]
    im = [field_ref[j, 1] for j in range(4)]
    re, im = filter_cols(re, im, high_ref, low_ref)
    for j in range(4):
        cos_v, sin_v = cos_ref[j], sin_ref[j]
        re[j], im[j] = re[j] * cos_v - im[j] * sin_v, im[j] * cos_v + re[j] * sin_v
        keep(j, re[j], im[j])
    re, im = filter_cols(re, im, high_ref, low_ref)
    for j in range(4):
        out_ref[j, 0] = re[j]
        out_ref[j, 1] = im[j]


def middle_source(cos_ref, sin_ref, field_ref, high_ref, low_ref, out_ref, mid_ref):
    def keep(j, re, im):
        mid_ref[j, 0] = re
        mid_ref[j, 1] = im

    middle_step(cos_ref, sin_ref, field_ref, high_ref, low_ref, out_ref, keep)


def middle_receiver(cos_ref, sin_ref, field_ref, high_ref, low_ref, mid_ref, out_ref, term_ref):
    def keep(j, re, im):
        term_ref[j] = mid_ref[j, 0] * re - mid_ref[j, 1] * im

    middle_step(cos_ref, sin_ref, field_ref, high_ref, low_ref, out_ref, keep)


def last_step(cos_ref, sin_ref, field_ref, high_ref, low_ref, keep):
    quarter = field_ref.shape[3]
    re = [field_ref[j, 0] for j in range(4)]
    im = [field_ref[j, 1] for j in range(4)]
    re, im = filter_rows(re, im, high_ref, low_ref)
    for j in range(4):
        span = pl.ds(j * quarter, quarter)
        cos_v, sin_v = cos_ref[:, span], sin_ref[:, span]
        keep(span, re[j] * cos_v - im[j] * sin_v, im[j] * cos_v + re[j] * sin_v)


def last_source(cos_ref, sin_ref, field_ref, high_ref, low_ref, source_ref):
    def keep(span, re, im):
        source_ref[0, 0, :, span] = re
        source_ref[1, 0, :, span] = im

    last_step(cos_ref, sin_ref, field_ref, high_ref, low_ref, keep)


def last_receiver(cos_ref, sin_ref, field_ref, high_ref, low_ref, source_ref, receiver_ref, term_ref):
    def keep(span, re, im):
        term_ref[span.start // span.size] = (
            source_ref[0, 0, :, span] * re - source_ref[1, 0, :, span] * im
        )
        receiver_ref[0, 0, :, span] = re
        receiver_ref[1, 0, :, span] = -im

    last_step(cos_ref, sin_ref, field_ref, high_ref, low_ref, keep)


def params():
    return pltpu.CompilerParams(vmem_limit_bytes=vmem_bytes, dimension_semantics=("arbitrary",))


def whole(shape):
    return pl.BlockSpec(shape, lambda i: (0,) * len(shape))


def swap(blocks):
    return lax.all_to_all(blocks, "row", split_axis=0, concat_axis=0, tiled=True)


def sum_strips(strips):
    count = strips.shape[0]
    me = lax.axis_index("freq")
    total = lax.dynamic_index_in_dim(strips, me, 0, keepdims=False)
    for shift in range(1, count):
        sent = lax.dynamic_index_in_dim(strips, (me + shift) % count, 0, keepdims=False)
        total = total + lax.ppermute(sent, "freq", [(i, (i + shift) % count) for i in range(count)])
    return total


def body(source_field, receiver_field, slowness, owner, freq_index):
    rows, width = source_field.shape[2:]
    row_count = lax.axis_size("row")
    freq_count = lax.axis_size("freq")
    height = rows * row_count
    cols = width // row_count
    quart_w = width // 4
    quart_h = height // 4
    more = row_count // 4
    omega = 2.0 * math.pi * (base_hertz + step_hertz * freq_index.astype(jnp.float32))

    def turning(slab):
        theta = slab * (omega[0] * dz_km)
        return jnp.cos(theta), jnp.sin(theta)

    def owned(depth):
        return jnp.where(lax.axis_index("freq") == owner[depth], slowness[0], 0.0)

    turned = swap(jnp.moveaxis(owned(0).reshape(rows, row_count, cols), 1, 0))
    piece_last = lax.psum_scatter(owned(1), "freq", scatter_dimension=0, tiled=True)
    source_field, turned = lax.optimization_barrier((source_field, turned))
    turned, piece_last = lax.optimization_barrier((turned, piece_last))
    piece = lax.psum_scatter(turned, "freq", scatter_dimension=0, tiled=True)
    receiver_field, piece = lax.optimization_barrier((receiver_field, piece))
    slab_first = lax.all_gather(piece, "freq", axis=0, tiled=True)
    piece_last, slab_first = lax.optimization_barrier((piece_last, slab_first))
    slab_last = lax.all_gather(piece_last, "freq", axis=0, tiled=True)
    turn_first = turning(slab_first.reshape(4, quart_h, cols))

    block_w = toeplitz_blocks(width, omega[0])
    block_h = block_w if height == width else toeplitz_blocks(height, omega[0])
    row_high, row_low = row_matrix(*block_w)
    col_high, col_low = column_matrix(*block_h)
    mat_w = whole((4, 2 * quart_w, 2 * quart_w))
    mat_h = whole((4, 2 * quart_h, 2 * quart_h))

    step = min(rows, 128)
    row_block = pl.BlockSpec((2, 1, step, width), lambda i: (0, 0, i, 0))
    quarter_block = pl.BlockSpec((4, 2, step, quart_w), lambda i: (0, 0, i, 0))
    line_block = pl.BlockSpec((step, width), lambda i: (i, 0))
    col_block = pl.BlockSpec((4, 2, quart_h, cols), lambda i: (0, 0, 0, 0))
    term_block = pl.BlockSpec((4, quart_h, cols), lambda i: (0, 0, 0))
    quarter_shape = jax.ShapeDtypeStruct((4, 2, rows, quart_w), jnp.float32)
    col_shape = jax.ShapeDtypeStruct((4, 2, quart_h, cols), jnp.float32)
    term_shape = jax.ShapeDtypeStruct((4, quart_h, cols), jnp.float32)
    strip_block = pl.BlockSpec((4, step, quart_w), lambda i: (0, i, 0))
    strip_shape = jax.ShapeDtypeStruct((4, rows, quart_w), jnp.float32)
    field_shape = jax.ShapeDtypeStruct(source_field.shape, jnp.float32)

    def first(field, sign):
        return pl.pallas_call(
            partial(first_kernel, sign),
            grid=(rows // step,),
            in_specs=[row_block, mat_w, mat_w],
            out_specs=quarter_block,
            out_shape=quarter_shape,
            compiler_params=params(),
        )(field, row_high, row_low)

    def to_cols(fields):
        if more > 1:
            fields = fields.reshape(4, 2, rows, more, cols)
            fields = jnp.moveaxis(fields, 3, 1).reshape(row_count, 2, rows, cols)
        fields = swap(fields)
        if more > 1:
            fields = fields.reshape(4, more, 2, rows, cols)
            fields = jnp.moveaxis(fields, 1, 2).reshape(4, 2, quart_h, cols)
        return fields

    def to_rows(fields):
        if more > 1:
            fields = fields.reshape(4, 2, more, rows, cols)
            fields = jnp.moveaxis(fields, 2, 1).reshape(row_count, 2, rows, cols)
        fields = swap(fields)
        if more > 1:
            fields = fields.reshape(4, more, 2, rows, cols)
            fields = jnp.moveaxis(fields, 1, 3).reshape(4, 2, rows, quart_w)
        return fields

    source = to_cols(first(source_field, 1.0))
    receiver = to_cols(first(receiver_field, -1.0))
    source, middle = pl.pallas_call(
        middle_source,
        grid=(1,),
        in_specs=[term_block, term_block, col_block, mat_h, mat_h],
        out_specs=[col_block, col_block],
        out_shape=[col_shape, col_shape],
        compiler_params=params(),
    )(*turn_first, source, col_high, col_low)
    source = to_rows(source)
    receiver, term = pl.pallas_call(
        middle_receiver,
        grid=(1,),
        in_specs=[term_block, term_block, col_block, mat_h, mat_h, col_block],
        out_specs=[col_block, term_block],
        out_shape=[col_shape, term_shape],
        compiler_params=params(),
    )(*turn_first, receiver, col_high, col_low, middle)
    receiver, term, slab_last = lax.optimization_barrier((receiver, term, slab_last))
    turn_last = turning(slab_last)
    receiver = to_rows(receiver)

    term = term.reshape(height, cols)
    if row_count == freq_count:
        part = lax.psum_scatter(term, "freq", scatter_dimension=0, tiled=True)
        pairs = [
            (r * freq_count + f, f * freq_count + r)
            for r in range(row_count)
            for f in range(freq_count)
        ]
        image_first = lax.ppermute(part, ("row", "freq"), pairs)
    else:
        term = lax.all_to_all(term, "row", split_axis=0, concat_axis=1, tiled=True)
        image_first = lax.psum_scatter(term, "freq", scatter_dimension=1, tiled=True)

    source_out = pl.pallas_call(
        last_source,
        grid=(rows // step,),
        in_specs=[line_block, line_block, quarter_block, mat_w, mat_w],
        out_specs=row_block,
        out_shape=field_shape,
        compiler_params=params(),
    )(*turn_last, source, row_high, row_low)
    receiver_out, term = pl.pallas_call(
        last_receiver,
        grid=(rows // step,),
        in_specs=[line_block, line_block, quarter_block, mat_w, mat_w, row_block],
        out_specs=[row_block, strip_block],
        out_shape=[field_shape, strip_shape],
        compiler_params=params(),
    )(*turn_last, receiver, row_high, row_low, source_out)
    if freq_count == 4:
        image_last = sum_strips(term)
    else:
        term = jnp.moveaxis(term, 0, 1).reshape(rows, width)
        image_last = lax.psum_scatter(term, "freq", scatter_dimension=1, tiled=True)
    return source_out, receiver_out, jnp.stack([image_first, image_last])


fused_vmem = 60 * 1024 * 1024
MESH = pl.DeviceIdType.MESH


def filter_table(length, count):
    quarter = length // 4
    offset = np.arange(1 - quarter, quarter)
    place = np.arange(quarter)
    delta = place[:, None] - place[None, :] + quarter - 1
    table = np.zeros((count, 4, 2, quarter, quarter), np.float32)
    kmax = math.pi / dx_km
    for slot in range(count):
        omega = 2.0 * math.pi * (base_hertz + step_hertz * slot)
        for k in range(4):
            kept = 4 * place + k
            signed = np.where(kept * 2 < length, kept, kept - length)
            square = (signed * (2.0 * math.pi / (length * dx_km))) ** 2
            amp = np.exp(-taper * square / kmax**2 - 1j * (dz_km / omega) * square) / length
            turns = (offset[:, None] * kept[None, :]) % length
            kernel = np.exp(2j * math.pi / length * turns) @ amp
            table[slot, k, 0] = kernel.real[delta]
            table[slot, k, 1] = kernel.imag[delta]
    return table


def turn_of(theta):
    square = theta * theta
    cos_v = 1.0 / 87178291200.0
    sin_v = 1.0 / 1307674368000.0
    cos_v = 1.0 / 479001600.0 - square * cos_v
    sin_v = 1.0 / 6227020800.0 - square * sin_v
    for even in (10, 8, 6, 4, 2, 0):
        cos_v = 1.0 / math.factorial(even) - square * cos_v
        sin_v = 1.0 / math.factorial(even + 1) - square * sin_v
    return cos_v, theta * sin_v


def row_pass(re, im, mats):
    step, quarter = re[0].shape
    re, im = butterfly(re, im, 1)
    out_r, out_i = [], []
    for k in range(4):
        turned = (4 - k) % 4
        high, low = halves(jnp.concatenate([re[k], im[k]], axis=1))
        out = dot(jnp.concatenate([high, low], axis=0), mats[turned])
        out = out[:step] + (out[step:] + dot(high, mats[4 + turned]))
        out_r.append(out[:, :quarter])
        out_i.append(out[:, quarter:])
    return butterfly(out_r, out_i, -1)


def col_pass(re, im, mats):
    quarter = re[0].shape[0]
    re, im = butterfly(re, im, -1)
    out_r, out_i = [], []
    for k in range(4):
        high, low = halves(jnp.concatenate([re[k], im[k]], axis=0))
        out = dot(mats[k], high) + (dot(mats[k], low) + dot(mats[4 + k], high))
        out_r.append(out[:quarter])
        out_i.append(out[quarter:])
    return butterfly(out_r, out_i, 1)


def wait_for(ref, sem):
    pltpu.make_async_copy(ref, ref, sem).wait()


def fused_kernel(
    step, late_steps, owner, slot, src_in, rec_in, slow_in, table_in, src_out, rec_out, img_out,
    field, mats, slab, early, cols, mid, store, masked, shared, piece, grid_first, grid_last,
    cos_first, sin_first, cos_last, sin_last, term_first, got_first, part_first, term_last, got_last, image,
    load_sem, store_sem, early_send, cols_recv, own_sem, late_send, lines_recv,
    shared_send, shared_recv, piece_send, piece_recv, depth_send, depth_recv, across_send, across_recv,
    first_send, first_recv, cross_send, cross_recv, last_send, last_recv,
):
    shot, row, freq = lax.axis_index("shot"), lax.axis_index("row"), lax.axis_index("freq")
    rows, width = slab.shape
    quarter = width // 4
    half = quarter // 2
    chunks = rows // step
    late_counts = [rows // size for size in late_steps]
    eighth = rows // 8
    chip, core = lax.div(row, 2), lax.rem(row, 2)
    row_peers = [(1 - chip) * 2 + core, (1 - chip) * 2 + 1 - core, chip * 2 + 1 - core]
    freq_peers = [lax.rem(freq + 1, 4), lax.rem(freq + 3, 4), lax.rem(freq + 2, 4)]

    def send(source, target, send_sem, recv_sem, device):
        pltpu.make_async_remote_copy(
            src_ref=source, dst_ref=target, send_sem=send_sem, recv_sem=recv_sem,
            device_id=device, device_id_type=MESH,
        ).start()

    def span(c, size=step):
        return pl.ds(pl.multiple_of(c * size, size), size)

    def pieces(values):
        return [
            jnp.concatenate([values[b][:, x * half : (x + 1) * half] for b in (core, core + 2)], axis=1)
            for x in range(2)
            for core in range(2)
        ]

    loads = [
        pltpu.make_async_copy(table_in, store, load_sem.at[1]),
        pltpu.make_async_copy(src_in.at[:, 0], field.at[0], load_sem.at[0]),
        pltpu.make_async_copy(slow_in.at[0], slab, load_sem.at[2]),
        pltpu.make_async_copy(rec_in.at[:, 0], field.at[1], load_sem.at[3]),
    ]
    for load in loads:
        load.start()

    barrier = pltpu.get_barrier_semaphore()
    peers = [(shot, peer, freq) for peer in row_peers] + [(shot, row, peer) for peer in freq_peers]
    for device in peers + [(1 - shot, row, freq)]:
        pl.semaphore_signal(barrier, inc=1, device_id=device, device_id_type=MESH)

    pl.semaphore_wait(barrier, 7)

    omega_dz = (2.0 * math.pi * dz_km) * (base_hertz + step_hertz * slot[0].astype(jnp.float32))

    def early_rows(which, c):
        place = span(c)
        re = [field[which, 0, place, j * quarter : (j + 1) * quarter] for j in range(4)]
        im = [field[which, 1, place, j * quarter : (j + 1) * quarter] for j in range(4)]
        if which == 0:
            im = [-v for v in im]
        re, im = row_pass(re, im, mats)
        re, im = pieces(re), pieces(im)
        for j in range(4):
            early[which, c, j, 0] = re[j]
            early[which, c, j, 1] = -im[j]

    def early_go(which, c):
        target = cols.at[which, row, :, span(c), :]
        for peer in row_peers:
            send(early.at[which, c, peer], target, early_send.at[which, c], cols_recv.at[which], (shot, peer, freq))
        pltpu.make_async_copy(early.at[which, c, row], target, own_sem.at[0, which]).start()

    def early_sent(which, c):
        wait_for(early.at[which, c, pl.ds(0, 3)], early_send.at[which, c])

    def late_go(which, c):
        place = span(c, late_steps[which])
        target = store.at[2 + which, row, :, place, :]
        for peer in row_peers:
            send(
                store.at[which, peer, :, place, :], target,
                late_send.at[which, c], lines_recv.at[which, c], (shot, peer, freq),
            )

    def late_sent(which, c):
        wait_for(store.at[which, pl.ds(0, 3), :, span(c, late_steps[which]), :], late_send.at[which, c])

    def share_go(depth):
        for peer in freq_peers:
            send(masked.at[depth, peer], shared.at[depth, freq], shared_send.at[depth], shared_recv.at[depth], (shot, row, peer))

    def share_sum(depth):
        shared[depth, freq] = masked[depth, freq]
        wait_for(shared.at[depth, pl.ds(0, 3)], shared_recv.at[depth])
        return (shared[depth, 0] + shared[depth, 1]) + (shared[depth, 2] + shared[depth, 3])

    def gather_go(depth, ref):
        for peer in freq_peers:
            send(ref.at[shot, freq], ref.at[shot, freq], depth_send.at[depth], depth_recv.at[depth, freq], (shot, row, peer))
        send(ref.at[shot, freq], ref.at[shot, freq], across_send.at[depth], across_recv.at[depth], (1 - shot, row, freq))

    def gather_end(depth, ref):
        for peer in freq_peers:
            block = ref.at[shot, peer]
            wait_for(block, depth_recv.at[depth, peer])
            send(block, block, across_send.at[depth], across_recv.at[depth], (1 - shot, row, freq))

    def gather_wait(depth, ref):
        wait_for(ref.at[1 - shot], across_recv.at[depth])

    loads[0].wait()
    which_slot = slot[0]
    for k in range(4):
        real_high, real_low = halves(store[which_slot, k, 0])
        imag_high, imag_low = halves(store[which_slot, k, 1])
        for at, real, imag in ((k, real_high, imag_high), (4 + k, real_low, imag_low)):
            mats[at, :quarter, :quarter] = real
            mats[at, quarter:, quarter:] = real
            mats[at, quarter:, :quarter] = imag
            mats[at, :quarter, quarter:] = -imag
    loads[1].wait()
    early_rows(0, 0)
    early_go(0, 0)
    loads[2].wait()
    for depth in range(2):
        mine = jnp.where(owner[depth] == freq, 1.0, 0.0)
        for k in range(4):
            base = pl.multiple_of((shot * 4 + k) * eighth, eighth)
            masked[depth, k] = slab[pl.ds(base, eighth), :] * mine
    share_go(0)

    @pl.loop(1, chunks)
    def _(c):
        early_rows(0, c)
        early_go(0, c)

    loads[3].wait()

    @pl.loop(0, chunks)
    def _(c):
        early_rows(1, c)

    total = share_sum(0)
    parts = pieces([total[:, b * quarter : (b + 1) * quarter] for b in range(4)])
    for j in range(4):
        piece[j] = parts[j]
    for peer in row_peers:
        send(piece.at[peer], grid_first.at[shot, freq, row], piece_send, piece_recv, (shot, peer, freq))
    grid_first[shot, freq, row] = piece[row]
    share_go(1)
    for c in range(chunks - 1):
        early_sent(0, c)
    early_go(1, 0)
    wait_for(grid_first.at[shot, freq, pl.ds(0, 3)], piece_recv)
    gather_go(0, grid_first)
    early_sent(0, chunks - 1)
    early_go(1, 1)

    def col_ready(which):
        wait_for(cols.at[which, 0], own_sem.at[0, which])
        wait_for(cols.at[which, pl.ds(0, 3)], cols_recv.at[which])

    def col_first(which):
        return col_pass([cols[which, j, 0] for j in range(4)], [cols[which, j, 1] for j in range(4)], mats)

    def turned(j, re, im):
        return re * cos_first[j] - im * sin_first[j], im * cos_first[j] + re * sin_first[j]

    def col_second(which, re, im):
        re, im = col_pass(re, im, mats)
        for j in range(4):
            store[which, j, 0] = re[j]
            store[which, j, 1] = im[j]
        pltpu.make_async_copy(store.at[which, row], store.at[2 + which, row], own_sem.at[1, which]).start()

    col_ready(0)
    re, im = col_first(0)
    for j in range(4):
        mid[j, 0] = re[j]
        mid[j, 1] = im[j]
    early_sent(1, 0)
    early_go(1, 2)
    gather_end(0, grid_first)
    grid_last[shot, freq] = share_sum(1)
    gather_go(1, grid_last)
    early_sent(1, 1)
    early_go(1, 3)
    gather_wait(0, grid_first)
    for j in range(4):
        theta = grid_first[:, :, j].reshape(rows, quarter) * omega_dz
        cos_first[j], sin_first[j] = turn_of(theta)
    re, im = [], []
    for j in range(4):
        real, imag = turned(j, mid[j, 0], mid[j, 1])
        mid[j, 0] = real
        mid[j, 1] = imag
        re.append(real)
        im.append(imag)
    col_second(0, re, im)
    for c in range(late_counts[0]):
        late_go(0, c)

    col_ready(1)
    re, im = col_first(1)
    for j in range(4):
        re[j], im[j] = turned(j, re[j], im[j])
        term = mid[j, 0] * re[j] - mid[j, 1] * im[j]
        for h in range(2):
            term_first[h, j] = term[:, h * half : (h + 1) * half]
    for h in range(2):
        peer = core + 2 * h

        @pl.when(peer != freq)
        def _(h=h, peer=peer):
            send(term_first.at[h], got_first.at[freq], first_send.at[h], first_recv.at[freq], (shot, row, peer))

    col_second(1, re, im)

    gather_end(1, grid_last)
    gather_wait(1, grid_last)
    cos_last[...], sin_last[...] = turn_of(grid_last[...].reshape(rows, width) * omega_dz)

    def final_rows(which, c):
        size = late_steps[which]
        place = span(c, size)
        wait_for(store.at[2 + which, pl.ds(0, 3), :, place, :], lines_recv.at[which, c])

        def gathered(b, part):
            lanes = slice((b // 2) * half, (b // 2 + 1) * half)
            return jnp.concatenate([store[2 + which, 2 * x + b % 2, part, place, lanes] for x in range(2)], axis=1)

        re = [gathered(b, 0) for b in range(4)]
        im = [-gathered(b, 1) for b in range(4)]
        re, im = row_pass(re, im, mats)
        for j in range(4):
            here = slice(j * quarter, (j + 1) * quarter)
            cos_v, sin_v = cos_last[place, here], sin_last[place, here]
            real = re[j] * cos_v + im[j] * sin_v
            imag = im[j] * cos_v - re[j] * sin_v
            if which == 0:
                imag = -imag
            else:
                term_last[c, j] = field[0, 0, place, here] * real + field[0, 1, place, here] * imag
            field[which, 0, place, here] = real
            field[which, 1, place, here] = imag
        out = (src_out, rec_out)[which]
        pltpu.make_async_copy(field.at[which, :, place, :], out.at[:, 0, place, :], store_sem.at[which]).start()

    for c in range(late_counts[0]):
        late_sent(0, c)
    for c in range(late_counts[1]):
        late_go(1, c)
    wait_for(store.at[0, 0], own_sem.at[1, 0])
    wait_for(store.at[1, 0], own_sem.at[1, 1])

    @pl.loop(0, late_counts[0])
    def _(c):
        final_rows(0, c)

    active = lax.rem(freq, 2) == core
    strip = pl.ds(pl.multiple_of(chip * half, half), half)

    @pl.when(active)
    def _():
        got_first[freq] = term_first[lax.div(freq, 2)]
        for peer in freq_peers:
            wait_for(got_first.at[peer], first_recv.at[peer])
        for a in range(4):
            part_first[a] = (got_first[0, a] + got_first[1, a]) + (got_first[2, a] + got_first[3, a])
        for peer in row_peers:
            send(part_first.at[peer], image.at[0, :, strip], cross_send, cross_recv.at[chip], (shot, peer, freq))
        image[0, :, strip] = part_first[row]

    @pl.loop(0, late_counts[1])
    def _(c):
        final_rows(1, c)
        for peer in freq_peers:
            send(term_last.at[c, peer], got_last.at[freq, c], last_send, last_recv.at[c], (shot, row, peer))

    got_last[freq] = term_last[:, freq]
    other = pl.ds(pl.multiple_of((1 - chip) * half, half), half)
    wait_for(image.at[0, :, other], cross_recv.at[1 - chip])

    @pl.when(active)
    def _():
        wait_for(part_first.at[pl.ds(0, 3)], cross_send)

    @pl.when(jnp.logical_not(active))
    def _():
        wait_for(image.at[0, :, strip], cross_recv.at[chip])

    pltpu.make_async_copy(image.at[0], img_out.at[0], store_sem.at[2]).start()

    @pl.loop(0, late_counts[1])
    def _(c):
        wait_for(got_last.at[pl.ds(0, 3), c], last_recv.at[c])
        image[1, span(c, late_steps[1]), :] = (got_last[0, c] + got_last[1, c]) + (got_last[2, c] + got_last[3, c])

    pltpu.make_async_copy(image.at[1], img_out.at[1], store_sem.at[3]).start()

    wait_for(piece.at[pl.ds(0, 3)], piece_send)
    for depth, ref in enumerate((grid_first, grid_last)):
        wait_for(masked.at[depth, pl.ds(0, 3)], shared_send.at[depth])
        wait_for(ref.at[0, pl.ds(0, 3)], depth_send.at[depth])
        wait_for(ref.at[0], across_send.at[depth])
    for c in (2, 3):
        early_sent(1, c)
    for c in range(late_counts[1]):
        late_sent(1, c)
    for h in range(2):

        @pl.when(core + 2 * h != freq)
        def _(h=h):
            wait_for(term_first.at[h], first_send.at[h])

    wait_for(term_last.at[:, pl.ds(0, 3)], last_send)
    wait_for(field.at[0], store_sem.at[0])
    wait_for(field.at[1], store_sem.at[1])
    wait_for(image.at[0], store_sem.at[2])
    wait_for(image.at[1], store_sem.at[3])


def fused_body(table, source_field, receiver_field, slowness, owner, freq_index):
    rows, width = source_field.shape[2:]
    quarter = width // 4
    chunks = 4
    step = rows // chunks
    late_steps = (rows // 4, rows // 8)

    def floats(*shape):
        return pltpu.VMEM(shape, jnp.float32)

    dma = pltpu.SemaphoreType.DMA
    block = (4, 2, rows, quarter)
    small = pl.BlockSpec(memory_space=pltpu.SMEM)
    any_spec = pl.BlockSpec(memory_space=pl.ANY)
    return pl.pallas_call(
        partial(fused_kernel, step, late_steps),
        out_shape=[
            jax.ShapeDtypeStruct(source_field.shape, jnp.float32),
            jax.ShapeDtypeStruct(source_field.shape, jnp.float32),
            jax.ShapeDtypeStruct((2, rows, quarter), jnp.float32),
        ],
        in_specs=[small] * 2 + [any_spec] * 4,
        out_specs=[any_spec] * 3,
        scratch_shapes=[
            floats(2, 2, rows, width),
            pltpu.VMEM((8, 2 * quarter, 2 * quarter), jnp.bfloat16),
            floats(rows, width),
            floats(2, chunks, 4, 2, step, quarter),
            floats(2, *block),
            floats(*block),
            floats(4, *block),
            floats(2, 4, rows // 8, width),
            floats(2, 4, rows // 8, width),
            floats(4, rows // 8, quarter),
            floats(2, 4, 4, rows // 8, quarter),
            floats(2, 4, rows // 8, width),
            floats(4, rows, quarter),
            floats(4, rows, quarter),
            floats(rows, width),
            floats(rows, width),
            floats(2, 4, rows, quarter // 2),
            floats(4, 4, rows, quarter // 2),
            floats(4, rows, quarter // 2),
            floats(8, 4, rows // 8, quarter),
            floats(4, 8, rows // 8, quarter),
            floats(2, rows, quarter),
            dma((4,)), dma((4,)), dma((2, chunks)), dma((2,)), dma((2, 2)), dma((2, 8)), dma((2, 8)),
            dma((2,)), dma((2,)), dma, dma, dma((2,)), dma((2, 4)), dma((2,)), dma((2,)),
            dma((2,)), dma((4,)), dma, dma((2,)), dma, dma((8,)),
        ],
        compiler_params=pltpu.CompilerParams(
            collective_id=0, has_side_effects=True, vmem_limit_bytes=fused_vmem
        ),
    )(owner, freq_index, source_field, receiver_field, slowness, table)


def solution(mesh):
    in_specs = (
        P(None, ("shot", "freq"), "row", None),
        P(None, ("shot", "freq"), "row", None),
        P("freq", "row", None),
        P(),
        P(("shot", "freq")),
    )
    out_specs = (
        P(None, ("shot", "freq"), "row", None),
        P(None, ("shot", "freq"), "row", None),
        P("shot", "row", "freq"),
    )
    sizes = tuple(mesh.shape[name] for name in ("shot", "row", "freq"))

    def whole_program(source_field, *rest):
        height, width = source_field.shape[2:]
        part = body
        if sizes == (2, 4, 4) and height == width and width % 1024 == 0:
            part = partial(fused_body, filter_table(width, sizes[2]))
        return jax.shard_map(part, mesh=mesh, in_specs=in_specs, out_specs=out_specs, check_vma=False)(
            source_field, *rest
        )

    return whole_program
```

```python
import math
from functools import partial

import jax
import jax.numpy as jnp
import numpy as np
from jax import lax
from jax.experimental import pallas as pl
from jax.experimental.pallas import tpu as pltpu
from jax.sharding import PartitionSpec as P

dz_km = 0.01
dx_km = 0.0125
base_hertz = 3.0
step_hertz = 4.0
taper = 0.5
vmem_bytes = 56 * 1024 * 1024


def split_high_low(value):
    high = lax.reduce_precision(value, 8, 7)
    return high.astype(jnp.bfloat16), (value - high).astype(jnp.bfloat16)


def toeplitz_blocks(length, omega):
    quarter = length // 4
    place = jnp.arange(quarter, dtype=jnp.int32)
    kept = 4 * place[None, :] + jnp.arange(4, dtype=jnp.int32)[:, None]
    signed = jnp.where(kept * 2 < length, kept, kept - length)
    square = (signed.astype(jnp.float32) * (2.0 * math.pi / (length * dx_km))) ** 2
    kmax = math.pi / dx_km
    damp = jnp.exp(-taper * square / (kmax * kmax)) / float(length)
    phase = (-dz_km / omega) * square
    amp_r = (damp * jnp.cos(phase))[:, None, :]
    amp_i = (damp * jnp.sin(phase))[:, None, :]
    turns = (kept[:, None, :] * place[None, :, None] % length).astype(jnp.float32)
    turns = turns * (2.0 * math.pi / length)
    cos_v = jnp.cos(turns)
    sin_v = jnp.sin(turns)
    left = jnp.concatenate([cos_v * amp_r - sin_v * amp_i, sin_v * amp_r + cos_v * amp_i], axis=2)
    right = jnp.concatenate(
        [jnp.concatenate([cos_v, sin_v], axis=2), jnp.concatenate([-sin_v, cos_v], axis=2)], axis=1
    )
    both = jnp.einsum("kbm,kcm->kbc", left, right, precision=lax.Precision.HIGHEST)
    return both[:, :, :quarter], both[:, :, quarter:]


def pack(real, imag, sign):
    top = jnp.concatenate([real, -sign * imag], axis=2)
    low = jnp.concatenate([sign * imag, real], axis=2)
    return split_high_low(jnp.concatenate([top, low], axis=1))


def column_matrix(real, imag):
    return pack(real, imag, 1.0)


def row_matrix(real, imag):
    turned_r = jnp.stack([real[0], real[3], real[2], real[1]])
    turned_i = jnp.stack([imag[0], imag[3], imag[2], imag[1]])
    return pack(turned_r, turned_i, -1.0)


def butterfly(re, im, sign):
    sum_r, dif_r = re[0] + re[2], re[0] - re[2]
    sum_i, dif_i = im[0] + im[2], im[0] - im[2]
    odd_r, gap_r = re[1] + re[3], re[1] - re[3]
    odd_i, gap_i = im[1] + im[3], im[1] - im[3]
    if sign < 0:
        gap_r, gap_i = -gap_r, -gap_i
    out_r = [sum_r + odd_r, dif_r - gap_i, sum_r - odd_r, dif_r + gap_i]
    out_i = [sum_i + odd_i, dif_i + gap_r, sum_i - odd_i, dif_i - gap_r]
    return out_r, out_i


def halves(value):
    high = value.astype(jnp.bfloat16)
    return high, (value - high.astype(jnp.float32)).astype(jnp.bfloat16)


def dot(left, right):
    return jnp.dot(left, right, preferred_element_type=jnp.float32)


def filter_rows(re, im, high_ref, low_ref):
    quarter = re[0].shape[1]
    re, im = butterfly(re, im, -1)
    out_r, out_i = [], []
    for k in range(4):
        high, low = halves(jnp.concatenate([re[k], im[k]], axis=1))
        out = dot(high, high_ref[k]) + (dot(low, high_ref[k]) + dot(high, low_ref[k]))
        out_r.append(out[:, :quarter])
        out_i.append(out[:, quarter:])
    return butterfly(out_r, out_i, 1)


def filter_cols(re, im, high_ref, low_ref):
    quarter = re[0].shape[0]
    re, im = butterfly(re, im, -1)
    out_r, out_i = [], []
    for k in range(4):
        high, low = halves(jnp.concatenate([re[k], im[k]], axis=0))
        out = dot(high_ref[k], high) + (dot(high_ref[k], low) + dot(low_ref[k], high))
        out_r.append(out[:quarter])
        out_i.append(out[quarter:])
    return butterfly(out_r, out_i, 1)


def first_kernel(sign, field_ref, high_ref, low_ref, out_ref):
    quarter = field_ref.shape[3] // 4
    re, im = [], []
    for j in range(4):
        span = pl.ds(j * quarter, quarter)
        re.append(field_ref[0, 0, :, span])
        im.append(sign * field_ref[1, 0, :, span])
    re, im = filter_rows(re, im, high_ref, low_ref)
    for j in range(4):
        out_ref[j, 0] = re[j]
        out_ref[j, 1] = im[j]


def middle_step(cos_ref, sin_ref, field_ref, high_ref, low_ref, out_ref, keep):
    re = [field_ref[j, 0] for j in range(4)]
    im = [field_ref[j, 1] for j in range(4)]
    re, im = filter_cols(re, im, high_ref, low_ref)
    for j in range(4):
        cos_v, sin_v = cos_ref[j], sin_ref[j]
        re[j], im[j] = re[j] * cos_v - im[j] * sin_v, im[j] * cos_v + re[j] * sin_v
        keep(j, re[j], im[j])
    re, im = filter_cols(re, im, high_ref, low_ref)
    for j in range(4):
        out_ref[j, 0] = re[j]
        out_ref[j, 1] = im[j]


def middle_source(cos_ref, sin_ref, field_ref, high_ref, low_ref, out_ref, mid_ref):
    def keep(j, re, im):
        mid_ref[j, 0] = re
        mid_ref[j, 1] = im

    middle_step(cos_ref, sin_ref, field_ref, high_ref, low_ref, out_ref, keep)


def middle_receiver(cos_ref, sin_ref, field_ref, high_ref, low_ref, mid_ref, out_ref, term_ref):
    def keep(j, re, im):
        term_ref[j] = mid_ref[j, 0] * re - mid_ref[j, 1] * im

    middle_step(cos_ref, sin_ref, field_ref, high_ref, low_ref, out_ref, keep)


def last_step(cos_ref, sin_ref, field_ref, high_ref, low_ref, keep):
    quarter = field_ref.shape[3]
    re = [field_ref[j, 0] for j in range(4)]
    im = [field_ref[j, 1] for j in range(4)]
    re, im = filter_rows(re, im, high_ref, low_ref)
    for j in range(4):
        span = pl.ds(j * quarter, quarter)
        cos_v, sin_v = cos_ref[:, span], sin_ref[:, span]
        keep(span, re[j] * cos_v - im[j] * sin_v, im[j] * cos_v + re[j] * sin_v)


def last_source(cos_ref, sin_ref, field_ref, high_ref, low_ref, source_ref):
    def keep(span, re, im):
        source_ref[0, 0, :, span] = re
        source_ref[1, 0, :, span] = im

    last_step(cos_ref, sin_ref, field_ref, high_ref, low_ref, keep)


def last_receiver(cos_ref, sin_ref, field_ref, high_ref, low_ref, source_ref, receiver_ref, term_ref):
    def keep(span, re, im):
        term_ref[span.start // span.size] = (
            source_ref[0, 0, :, span] * re - source_ref[1, 0, :, span] * im
        )
        receiver_ref[0, 0, :, span] = re
        receiver_ref[1, 0, :, span] = -im

    last_step(cos_ref, sin_ref, field_ref, high_ref, low_ref, keep)


def params():
    return pltpu.CompilerParams(vmem_limit_bytes=vmem_bytes, dimension_semantics=("arbitrary",))


def whole(shape):
    return pl.BlockSpec(shape, lambda i: (0,) * len(shape))


def swap(blocks):
    return lax.all_to_all(blocks, "row", split_axis=0, concat_axis=0, tiled=True)


def sum_strips(strips):
    count = strips.shape[0]
    me = lax.axis_index("freq")
    total = lax.dynamic_index_in_dim(strips, me, 0, keepdims=False)
    for shift in range(1, count):
        sent = lax.dynamic_index_in_dim(strips, (me + shift) % count, 0, keepdims=False)
        total = total + lax.ppermute(sent, "freq", [(i, (i + shift) % count) for i in range(count)])
    return total


def body(source_field, receiver_field, slowness, owner, freq_index):
    rows, width = source_field.shape[2:]
    row_count = lax.axis_size("row")
    freq_count = lax.axis_size("freq")
    height = rows * row_count
    cols = width // row_count
    quart_w = width // 4
    quart_h = height // 4
    more = row_count // 4
    omega = 2.0 * math.pi * (base_hertz + step_hertz * freq_index.astype(jnp.float32))

    def turning(slab):
        theta = slab * (omega[0] * dz_km)
        return jnp.cos(theta), jnp.sin(theta)

    def owned(depth):
        return jnp.where(lax.axis_index("freq") == owner[depth], slowness[0], 0.0)

    turned = swap(jnp.moveaxis(owned(0).reshape(rows, row_count, cols), 1, 0))
    piece_last = lax.psum_scatter(owned(1), "freq", scatter_dimension=0, tiled=True)
    source_field, turned = lax.optimization_barrier((source_field, turned))
    turned, piece_last = lax.optimization_barrier((turned, piece_last))
    piece = lax.psum_scatter(turned, "freq", scatter_dimension=0, tiled=True)
    receiver_field, piece = lax.optimization_barrier((receiver_field, piece))
    slab_first = lax.all_gather(piece, "freq", axis=0, tiled=True)
    piece_last, slab_first = lax.optimization_barrier((piece_last, slab_first))
    slab_last = lax.all_gather(piece_last, "freq", axis=0, tiled=True)
    turn_first = turning(slab_first.reshape(4, quart_h, cols))

    block_w = toeplitz_blocks(width, omega[0])
    block_h = block_w if height == width else toeplitz_blocks(height, omega[0])
    row_high, row_low = row_matrix(*block_w)
    col_high, col_low = column_matrix(*block_h)
    mat_w = whole((4, 2 * quart_w, 2 * quart_w))
    mat_h = whole((4, 2 * quart_h, 2 * quart_h))

    step = min(rows, 128)
    row_block = pl.BlockSpec((2, 1, step, width), lambda i: (0, 0, i, 0))
    quarter_block = pl.BlockSpec((4, 2, step, quart_w), lambda i: (0, 0, i, 0))
    line_block = pl.BlockSpec((step, width), lambda i: (i, 0))
    col_block = pl.BlockSpec((4, 2, quart_h, cols), lambda i: (0, 0, 0, 0))
    term_block = pl.BlockSpec((4, quart_h, cols), lambda i: (0, 0, 0))
    quarter_shape = jax.ShapeDtypeStruct((4, 2, rows, quart_w), jnp.float32)
    col_shape = jax.ShapeDtypeStruct((4, 2, quart_h, cols), jnp.float32)
    term_shape = jax.ShapeDtypeStruct((4, quart_h, cols), jnp.float32)
    strip_block = pl.BlockSpec((4, step, quart_w), lambda i: (0, i, 0))
    strip_shape = jax.ShapeDtypeStruct((4, rows, quart_w), jnp.float32)
    field_shape = jax.ShapeDtypeStruct(source_field.shape, jnp.float32)

    def first(field, sign):
        return pl.pallas_call(
            partial(first_kernel, sign),
            grid=(rows // step,),
            in_specs=[row_block, mat_w, mat_w],
            out_specs=quarter_block,
            out_shape=quarter_shape,
            compiler_params=params(),
        )(field, row_high, row_low)

    def to_cols(fields):
        if more > 1:
            fields = fields.reshape(4, 2, rows, more, cols)
            fields = jnp.moveaxis(fields, 3, 1).reshape(row_count, 2, rows, cols)
        fields = swap(fields)
        if more > 1:
            fields = fields.reshape(4, more, 2, rows, cols)
            fields = jnp.moveaxis(fields, 1, 2).reshape(4, 2, quart_h, cols)
        return fields

    def to_rows(fields):
        if more > 1:
            fields = fields.reshape(4, 2, more, rows, cols)
            fields = jnp.moveaxis(fields, 2, 1).reshape(row_count, 2, rows, cols)
        fields = swap(fields)
        if more > 1:
            fields = fields.reshape(4, more, 2, rows, cols)
            fields = jnp.moveaxis(fields, 1, 3).reshape(4, 2, rows, quart_w)
        return fields

    source = to_cols(first(source_field, 1.0))
    receiver = to_cols(first(receiver_field, -1.0))
    source, middle = pl.pallas_call(
        middle_source,
        grid=(1,),
        in_specs=[term_block, term_block, col_block, mat_h, mat_h],
        out_specs=[col_block, col_block],
        out_shape=[col_shape, col_shape],
        compiler_params=params(),
    )(*turn_first, source, col_high, col_low)
    source = to_rows(source)
    receiver, term = pl.pallas_call(
        middle_receiver,
        grid=(1,),
        in_specs=[term_block, term_block, col_block, mat_h, mat_h, col_block],
        out_specs=[col_block, term_block],
        out_shape=[col_shape, term_shape],
        compiler_params=params(),
    )(*turn_first, receiver, col_high, col_low, middle)
    receiver, term, slab_last = lax.optimization_barrier((receiver, term, slab_last))
    turn_last = turning(slab_last)
    receiver = to_rows(receiver)

    term = term.reshape(height, cols)
    if row_count == freq_count:
        part = lax.psum_scatter(term, "freq", scatter_dimension=0, tiled=True)
        pairs = [
            (r * freq_count + f, f * freq_count + r)
            for r in range(row_count)
            for f in range(freq_count)
        ]
        image_first = lax.ppermute(part, ("row", "freq"), pairs)
    else:
        term = lax.all_to_all(term, "row", split_axis=0, concat_axis=1, tiled=True)
        image_first = lax.psum_scatter(term, "freq", scatter_dimension=1, tiled=True)

    source_out = pl.pallas_call(
        last_source,
        grid=(rows // step,),
        in_specs=[line_block, line_block, quarter_block, mat_w, mat_w],
        out_specs=row_block,
        out_shape=field_shape,
        compiler_params=params(),
    )(*turn_last, source, row_high, row_low)
    receiver_out, term = pl.pallas_call(
        last_receiver,
        grid=(rows // step,),
        in_specs=[line_block, line_block, quarter_block, mat_w, mat_w, row_block],
        out_specs=[row_block, strip_block],
        out_shape=[field_shape, strip_shape],
        compiler_params=params(),
    )(*turn_last, receiver, row_high, row_low, source_out)
    if freq_count == 4:
        image_last = sum_strips(term)
    else:
        term = jnp.moveaxis(term, 0, 1).reshape(rows, width)
        image_last = lax.psum_scatter(term, "freq", scatter_dimension=1, tiled=True)
    return source_out, receiver_out, jnp.stack([image_first, image_last])


fused_vmem = 60 * 1024 * 1024
MESH = pl.DeviceIdType.MESH


def filter_table(length, count):
    quarter = length // 4
    offset = np.arange(2 * quarter)
    offset = np.where(offset < quarter, -offset, 2 * quarter - offset)
    place = np.arange(quarter)
    table = np.zeros((count, 8, 2 * quarter), np.float32)
    kmax = math.pi / dx_km
    for slot in range(count):
        omega = 2.0 * math.pi * (base_hertz + step_hertz * slot)
        for k in range(4):
            kept = 4 * place + k
            signed = np.where(kept * 2 < length, kept, kept - length)
            square = (signed * (2.0 * math.pi / (length * dx_km))) ** 2
            amp = np.exp(-taper * square / kmax**2 - 1j * (dz_km / omega) * square) / length
            turns = (offset[:, None] * kept[None, :]) % length
            kernel = np.exp(2j * math.pi / length * turns) @ amp
            table[slot, k] = kernel.real
            table[slot, 4 + k] = kernel.imag
    return table


def turn_of(theta):
    square = theta * theta
    cos_v = 1.0 / 87178291200.0
    sin_v = 1.0 / 1307674368000.0
    cos_v = 1.0 / 479001600.0 - square * cos_v
    sin_v = 1.0 / 6227020800.0 - square * sin_v
    for even in (10, 8, 6, 4, 2, 0):
        cos_v = 1.0 / math.factorial(even) - square * cos_v
        sin_v = 1.0 / math.factorial(even + 1) - square * sin_v
    return cos_v, theta * sin_v


def row_pass(re, im, mats):
    step, quarter = re[0].shape
    re, im = butterfly(re, im, 1)
    out_r, out_i = [], []
    for k in range(4):
        turned = (4 - k) % 4
        high, low = halves(jnp.concatenate([re[k], im[k]], axis=1))
        out = dot(jnp.concatenate([high, low], axis=0), mats[turned])
        out = out[:step] + (out[step:] + dot(high, mats[4 + turned]))
        out_r.append(out[:, :quarter])
        out_i.append(out[:, quarter:])
    return butterfly(out_r, out_i, -1)


def col_pass(re, im, mats):
    quarter = re[0].shape[0]
    re, im = butterfly(re, im, -1)
    out_r, out_i = [], []
    for k in range(4):
        high, low = halves(jnp.concatenate([re[k], im[k]], axis=0))
        out = dot(mats[k], high) + (dot(mats[k], low) + dot(mats[4 + k], high))
        out_r.append(out[:quarter])
        out_i.append(out[quarter:])
    return butterfly(out_r, out_i, 1)


def wait_for(ref, sem):
    pltpu.make_async_copy(ref, ref, sem).wait()


def fused_kernel(
    step, late_step, tail_step, owner, slot, src_in, rec_in, slow_in, table_in, src_out, rec_out, img_out,
    field, table, mats, slab, early, cols, mid, store, masked, shared, piece, grid_first, grid_last,
    cos_first, sin_first, cos_last, sin_last, term_first, got_first, part_first, term_last, got_last, image,
    load_sem, store_sem, early_send, cols_recv, own_sem, late_send, lines_recv,
    shared_send, shared_recv, piece_send, piece_recv, depth_send, depth_recv, across_send, across_recv,
    first_send, first_recv, cross_send, cross_recv, last_send, last_recv,
):
    shot, row, freq = lax.axis_index("shot"), lax.axis_index("row"), lax.axis_index("freq")
    rows, width = slab.shape
    quarter = width // 4
    half = quarter // 2
    chunks = rows // step
    late_count = rows // late_step
    tail_count = late_step // tail_step
    eighth = rows // 8
    chip, core = lax.div(row, 2), lax.rem(row, 2)
    row_peers = [(1 - chip) * 2 + core, (1 - chip) * 2 + 1 - core, chip * 2 + 1 - core]
    freq_peers = [lax.rem(freq + 1, 4), lax.rem(freq + 3, 4), lax.rem(freq + 2, 4)]

    def send(source, target, send_sem, recv_sem, device):
        pltpu.make_async_remote_copy(
            src_ref=source, dst_ref=target, send_sem=send_sem, recv_sem=recv_sem,
            device_id=device, device_id_type=MESH,
        ).start()

    def span(c, size=step):
        return pl.ds(pl.multiple_of(c * size, size), size)

    def tail_span(c):
        return pl.ds(pl.multiple_of(rows - late_step + c * tail_step, tail_step), tail_step)

    def pieces(values):
        return [
            jnp.concatenate([values[b][:, x * half : (x + 1) * half] for b in (core, core + 2)], axis=1)
            for x in range(2)
            for core in range(2)
        ]

    loads = [
        pltpu.make_async_copy(table_in, table, load_sem.at[1]),
        pltpu.make_async_copy(src_in.at[:, 0], field.at[0], load_sem.at[0]),
        pltpu.make_async_copy(slow_in.at[0], slab, load_sem.at[2]),
        pltpu.make_async_copy(rec_in.at[:, 0], field.at[1], load_sem.at[3]),
    ]
    for load in loads:
        load.start()

    barrier = pltpu.get_barrier_semaphore()
    peers = [(shot, peer, freq) for peer in row_peers] + [(shot, row, peer) for peer in freq_peers]
    for device in peers + [(1 - shot, row, freq)]:
        pl.semaphore_signal(barrier, inc=1, device_id=device, device_id_type=MESH)

    pl.semaphore_wait(barrier, 7)

    omega_dz = (2.0 * math.pi * dz_km) * (base_hertz + step_hertz * slot[0].astype(jnp.float32))

    def early_rows(which, c):
        place = span(c)
        re = [field[which, 0, place, j * quarter : (j + 1) * quarter] for j in range(4)]
        im = [field[which, 1, place, j * quarter : (j + 1) * quarter] for j in range(4)]
        if which == 0:
            im = [-v for v in im]
        re, im = row_pass(re, im, mats)
        re, im = pieces(re), pieces(im)
        for j in range(4):
            early[which, c, j, 0] = re[j]
            early[which, c, j, 1] = -im[j]

    def early_go(which, c):
        target = cols.at[which, row, :, span(c), :]
        for peer in row_peers:
            send(early.at[which, c, peer], target, early_send.at[which], cols_recv.at[which], (shot, peer, freq))
        pltpu.make_async_copy(early.at[which, c, row], target, own_sem.at[0, which]).start()

    def late_go(which, place, piece_no):
        target = store.at[2 + which, row, :, place, :]
        for peer in row_peers:
            send(
                store.at[which, peer, :, place, :], target,
                late_send.at[which], lines_recv.at[which, piece_no], (shot, peer, freq),
            )

    def share_go(depth):
        for peer in freq_peers:
            send(masked.at[depth, peer], shared.at[depth, freq], shared_send.at[depth], shared_recv.at[depth], (shot, row, peer))

    def share_sum(depth):
        shared[depth, freq] = masked[depth, freq]
        wait_for(shared.at[depth, pl.ds(0, 3)], shared_recv.at[depth])
        return (shared[depth, 0] + shared[depth, 1]) + (shared[depth, 2] + shared[depth, 3])

    def gather_go(depth, ref):
        for peer in freq_peers:
            send(ref.at[shot, freq], ref.at[shot, freq], depth_send.at[depth], depth_recv.at[depth, freq], (shot, row, peer))
        send(ref.at[shot, freq], ref.at[shot, freq], across_send.at[depth], across_recv.at[depth], (1 - shot, row, freq))

    def gather_end(depth, ref):
        for peer in freq_peers:
            block = ref.at[shot, peer]
            wait_for(block, depth_recv.at[depth, peer])
            send(block, block, across_send.at[depth], across_recv.at[depth], (1 - shot, row, freq))

    def gather_wait(depth, ref):
        wait_for(ref.at[1 - shot], across_recv.at[depth])

    loads[0].wait()
    kernels = table[slot[0]]

    def toeplitz(i):
        wide = jnp.broadcast_to(kernels[i : i + 1], (half, 2 * quarter))
        turned_rows = pltpu.roll(wide, 0, 1, stride=1, stride_axis=0)
        return [halves(turned_rows[:, n * half : (n + 1) * half]) for n in (0, 1, 3)]

    for k in range(4):
        reals, imags = toeplitz(k), toeplitz(4 + k)
        for r, c, n in ((0, 0, 0), (0, half, 1), (half, 0, 2), (half, half, 0)):
            near, far = slice(r, r + half), slice(quarter + r, quarter + r + half)
            near_c, far_c = slice(c, c + half), slice(quarter + c, quarter + c + half)
            for at, real, imag in zip((k, 4 + k), reals[n], imags[n]):
                mats[at, near, near_c] = real
                mats[at, far, far_c] = real
                mats[at, far, near_c] = imag
                mats[at, near, far_c] = -imag
    loads[1].wait()
    early_rows(0, 0)
    early_go(0, 0)
    loads[2].wait()
    for depth in range(2):
        mine = jnp.where(owner[depth] == freq, 1.0, 0.0)
        for k in range(4):
            base = pl.multiple_of((shot * 4 + k) * eighth, eighth)
            masked[depth, k] = slab[pl.ds(base, eighth), :] * mine
    share_go(0)

    @pl.loop(1, chunks)
    def _(c):
        early_rows(0, c)
        early_go(0, c)

    loads[3].wait()

    @pl.loop(0, chunks)
    def _(c):
        early_rows(1, c)

    total = share_sum(0)
    parts = pieces([total[:, b * quarter : (b + 1) * quarter] for b in range(4)])
    for j in range(4):
        piece[j] = parts[j]
    for peer in row_peers:
        send(piece.at[peer], grid_first.at[shot, freq, row], piece_send, piece_recv, (shot, peer, freq))
    grid_first[shot, freq, row] = piece[row]
    share_go(1)
    for c in range(chunks):
        early_go(1, c)
    wait_for(grid_first.at[shot, freq, pl.ds(0, 3)], piece_recv)
    gather_go(0, grid_first)

    def col_ready(which):
        wait_for(cols.at[which, 0], own_sem.at[0, which])
        wait_for(cols.at[which, pl.ds(0, 3)], cols_recv.at[which])

    def col_first(which):
        return col_pass([cols[which, j, 0] for j in range(4)], [cols[which, j, 1] for j in range(4)], mats)

    def turned(j, re, im):
        return re * cos_first[j] - im * sin_first[j], im * cos_first[j] + re * sin_first[j]

    def col_second(which, re, im):
        re, im = col_pass(re, im, mats)
        for j in range(4):
            store[which, j, 0] = re[j]
            store[which, j, 1] = im[j]
        pltpu.make_async_copy(store.at[which, row], store.at[2 + which, row], own_sem.at[1, which]).start()

    col_ready(0)
    re, im = col_first(0)
    for j in range(4):
        mid[j, 0] = re[j]
        mid[j, 1] = im[j]
    gather_end(0, grid_first)
    grid_last[shot, freq] = share_sum(1)
    gather_go(1, grid_last)
    gather_wait(0, grid_first)
    for j in range(4):
        theta = grid_first[:, :, j].reshape(rows, quarter) * omega_dz
        cos_first[j], sin_first[j] = turn_of(theta)
    re, im = [], []
    for j in range(4):
        real, imag = turned(j, mid[j, 0], mid[j, 1])
        mid[j, 0] = real
        mid[j, 1] = imag
        re.append(real)
        im.append(imag)
    col_second(0, re, im)
    for c in range(2):
        late_go(0, span(c, rows // 2), c)

    col_ready(1)
    re, im = col_first(1)
    for j in range(4):
        re[j], im[j] = turned(j, re[j], im[j])
        term = mid[j, 0] * re[j] - mid[j, 1] * im[j]
        for h in range(2):
            term_first[h, j] = term[:, h * half : (h + 1) * half]
    for h in range(2):
        peer = core + 2 * h

        @pl.when(peer != freq)
        def _(h=h, peer=peer):
            send(term_first.at[h], got_first.at[freq], first_send.at[h], first_recv.at[freq], (shot, row, peer))

    col_second(1, re, im)

    gather_end(1, grid_last)
    gather_wait(1, grid_last)
    cos_last[...], sin_last[...] = turn_of(grid_last[...].reshape(rows, width) * omega_dz)

    def final_rows(which, place, piece_no):
        wait_for(store.at[2 + which, pl.ds(0, 3), :, place, :], lines_recv.at[which, piece_no])

        def gathered(b, part):
            lanes = slice((b // 2) * half, (b // 2 + 1) * half)
            return jnp.concatenate([store[2 + which, 2 * x + b % 2, part, place, lanes] for x in range(2)], axis=1)

        re = [gathered(b, 0) for b in range(4)]
        im = [-gathered(b, 1) for b in range(4)]
        re, im = row_pass(re, im, mats)
        for j in range(4):
            here = slice(j * quarter, (j + 1) * quarter)
            cos_v, sin_v = cos_last[place, here], sin_last[place, here]
            real = re[j] * cos_v + im[j] * sin_v
            imag = im[j] * cos_v - re[j] * sin_v
            if which == 0:
                imag = -imag
            else:
                term_last[j, place, :] = field[0, 0, place, here] * real + field[0, 1, place, here] * imag
            field[which, 0, place, here] = real
            field[which, 1, place, here] = imag
        out = (src_out, rec_out)[which]
        pltpu.make_async_copy(field.at[which, :, place, :], out.at[:, 0, place, :], store_sem.at[which]).start()

    for c in range(late_count - 1):
        late_go(1, span(c, late_step), c)
    for c in range(tail_count):
        late_go(1, tail_span(c), late_count + c)
    wait_for(store.at[0, 0], own_sem.at[1, 0])
    wait_for(store.at[1, 0], own_sem.at[1, 1])

    @pl.loop(0, 2)
    def _(c):
        final_rows(0, span(c, rows // 2), c)

    active = lax.rem(freq, 2) == core
    strip = pl.ds(pl.multiple_of(chip * half, half), half)

    @pl.when(active)
    def _():
        got_first[freq] = term_first[lax.div(freq, 2)]
        for peer in freq_peers:
            wait_for(got_first.at[peer], first_recv.at[peer])
        for a in range(4):
            part_first[a] = (got_first[0, a] + got_first[1, a]) + (got_first[2, a] + got_first[3, a])
        for peer in row_peers:
            send(part_first.at[peer], image.at[0, :, strip], cross_send, cross_recv.at[chip], (shot, peer, freq))
        image[0, :, strip] = part_first[row]

    def last_rows(place, piece_no):
        final_rows(1, place, piece_no)
        for peer in freq_peers:
            send(
                term_last.at[peer, place, :], got_last.at[freq, place, :],
                last_send, last_recv.at[piece_no], (shot, row, peer),
            )

    @pl.loop(0, late_count - 1)
    def _(c):
        last_rows(span(c, late_step), c)

    @pl.loop(0, tail_count)
    def _(c):
        last_rows(tail_span(c), late_count + c)

    got_last[freq] = term_last[freq]
    other = pl.ds(pl.multiple_of((1 - chip) * half, half), half)
    wait_for(image.at[0, :, other], cross_recv.at[1 - chip])

    @pl.when(active)
    def _():
        wait_for(part_first.at[pl.ds(0, 3)], cross_send)

    @pl.when(jnp.logical_not(active))
    def _():
        wait_for(image.at[0, :, strip], cross_recv.at[chip])

    pltpu.make_async_copy(image.at[0], img_out.at[0], store_sem.at[2]).start()

    def last_sum(place, piece_no):
        wait_for(got_last.at[pl.ds(0, 3), place, :], last_recv.at[piece_no])
        image[1, place, :] = (got_last[0, place, :] + got_last[1, place, :]) + (
            got_last[2, place, :] + got_last[3, place, :]
        )

    @pl.loop(0, late_count - 1)
    def _(c):
        last_sum(span(c, late_step), c)

    @pl.loop(0, tail_count)
    def _(c):
        last_sum(tail_span(c), late_count + c)

    pltpu.make_async_copy(image.at[1], img_out.at[1], store_sem.at[3]).start()

    wait_for(piece.at[pl.ds(0, 3)], piece_send)
    for depth, ref in enumerate((grid_first, grid_last)):
        wait_for(masked.at[depth, pl.ds(0, 3)], shared_send.at[depth])
        wait_for(ref.at[0, pl.ds(0, 3)], depth_send.at[depth])
        wait_for(ref.at[0], across_send.at[depth])
    for which in range(2):
        wait_for(early.at[which, :, pl.ds(0, 3)], early_send.at[which])
        wait_for(store.at[which, pl.ds(0, 3)], late_send.at[which])
    for h in range(2):

        @pl.when(core + 2 * h != freq)
        def _(h=h):
            wait_for(term_first.at[h], first_send.at[h])

    wait_for(term_last.at[pl.ds(0, 3)], last_send)
    wait_for(field.at[0], store_sem.at[0])
    wait_for(field.at[1], store_sem.at[1])
    wait_for(image.at[0], store_sem.at[2])
    wait_for(image.at[1], store_sem.at[3])


def copy_kernel(count, *refs):
    places, outs, holds = refs[:count], refs[count : 2 * count], refs[2 * count : 3 * count]
    load_sem, store_sem = refs[3 * count :]
    loads = [pltpu.make_async_copy(places[i], holds[i], load_sem.at[i]) for i in range(count)]
    stores = [pltpu.make_async_copy(holds[i], outs[i], store_sem.at[i]) for i in range(count)]
    for load in loads:
        load.start()
    for load, store in zip(loads, stores):
        load.wait()
        store.start()
    for store in stores:
        store.wait()


def copied(arrays):
    any_spec = pl.BlockSpec(memory_space=pl.ANY)
    count = len(arrays)
    return pl.pallas_call(
        partial(copy_kernel, count),
        out_shape=[jax.ShapeDtypeStruct(a.shape, a.dtype) for a in arrays],
        in_specs=[any_spec] * count,
        out_specs=[any_spec] * count,
        scratch_shapes=[pltpu.VMEM(a.shape, a.dtype) for a in arrays] + [pltpu.SemaphoreType.DMA((count,))] * 2,
        compiler_params=pltpu.CompilerParams(vmem_limit_bytes=fused_vmem),
    )(*arrays)


def fused_body(table, source_field, receiver_field, slowness, owner, freq_index):
    rows, width = source_field.shape[2:]
    quarter = width // 4
    chunks = 8
    step = rows // chunks
    late_step = rows // 8
    tail_step = late_step // 1

    def floats(*shape):
        return pltpu.VMEM(shape, jnp.float32)

    dma = pltpu.SemaphoreType.DMA
    block = (4, 2, rows, quarter)
    small = pl.BlockSpec(memory_space=pltpu.SMEM)
    any_spec = pl.BlockSpec(memory_space=pl.ANY)
    outs = pl.pallas_call(
        partial(fused_kernel, step, late_step, tail_step),
        out_shape=[
            jax.ShapeDtypeStruct(source_field.shape, jnp.float32),
            jax.ShapeDtypeStruct(source_field.shape, jnp.float32),
            jax.ShapeDtypeStruct((2, rows, quarter), jnp.float32),
        ],
        in_specs=[small] * 2 + [any_spec] * 4,
        out_specs=[any_spec] * 3,
        scratch_shapes=[
            floats(2, 2, rows, width),
            floats(*table.shape),
            pltpu.VMEM((8, 2 * quarter, 2 * quarter), jnp.bfloat16),
            floats(rows, width),
            floats(2, chunks, 4, 2, step, quarter),
            floats(2, *block),
            floats(*block),
            floats(4, *block),
            floats(2, 4, rows // 8, width),
            floats(2, 4, rows // 8, width),
            floats(4, rows // 8, quarter),
            floats(2, 4, 4, rows // 8, quarter),
            floats(2, 4, rows // 8, width),
            floats(4, rows, quarter),
            floats(4, rows, quarter),
            floats(rows, width),
            floats(rows, width),
            floats(2, 4, rows, quarter // 2),
            floats(4, 4, rows, quarter // 2),
            floats(4, rows, quarter // 2),
            floats(4, rows, quarter),
            floats(4, rows, quarter),
            floats(2, rows, quarter),
            dma((6,)), dma((4,)), dma((2,)), dma((2,)), dma((2, 2)), dma((2,)), dma((2, 16)),
            dma((2,)), dma((2,)), dma, dma, dma((2,)), dma((2, 4)), dma((2,)), dma((2,)),
            dma((2,)), dma((4,)), dma, dma((2,)), dma, dma((16,)),
        ],
        compiler_params=pltpu.CompilerParams(
            collective_id=0, has_side_effects=True, vmem_limit_bytes=fused_vmem
        ),
    )(owner, freq_index, source_field, receiver_field, slowness, table)
    return tuple(copied(outs))


def solution(mesh):
    in_specs = (
        P(None, ("shot", "freq"), "row", None),
        P(None, ("shot", "freq"), "row", None),
        P("freq", "row", None),
        P(),
        P(("shot", "freq")),
    )
    out_specs = (
        P(None, ("shot", "freq"), "row", None),
        P(None, ("shot", "freq"), "row", None),
        P("shot", "row", "freq"),
    )
    sizes = tuple(mesh.shape[name] for name in ("shot", "row", "freq"))

    def whole_program(source_field, *rest):
        height, width = source_field.shape[2:]
        part = body
        if sizes == (2, 4, 4) and height == width and width % 1024 == 0:
            part = partial(fused_body, filter_table(width, sizes[2]))
        return jax.shard_map(part, mesh=mesh, in_specs=in_specs, out_specs=out_specs, check_vma=False)(
            source_field, *rest
        )

    return whole_program
```

```python
import math
from functools import partial

import jax
import jax.numpy as jnp
import numpy as np
from jax import lax
from jax.experimental import pallas as pl
from jax.experimental.pallas import tpu as pltpu
from jax.sharding import PartitionSpec as P

dz_km = 0.01
dx_km = 0.0125
base_hertz = 3.0
step_hertz = 4.0
taper = 0.5
vmem_bytes = 56 * 1024 * 1024


def split_high_low(value):
    high = lax.reduce_precision(value, 8, 7)
    return high.astype(jnp.bfloat16), (value - high).astype(jnp.bfloat16)


def toeplitz_blocks(length, omega):
    quarter = length // 4
    place = jnp.arange(quarter, dtype=jnp.int32)
    kept = 4 * place[None, :] + jnp.arange(4, dtype=jnp.int32)[:, None]
    signed = jnp.where(kept * 2 < length, kept, kept - length)
    square = (signed.astype(jnp.float32) * (2.0 * math.pi / (length * dx_km))) ** 2
    kmax = math.pi / dx_km
    damp = jnp.exp(-taper * square / (kmax * kmax)) / float(length)
    phase = (-dz_km / omega) * square
    amp_r = (damp * jnp.cos(phase))[:, None, :]
    amp_i = (damp * jnp.sin(phase))[:, None, :]
    turns = (kept[:, None, :] * place[None, :, None] % length).astype(jnp.float32)
    turns = turns * (2.0 * math.pi / length)
    cos_v = jnp.cos(turns)
    sin_v = jnp.sin(turns)
    left = jnp.concatenate([cos_v * amp_r - sin_v * amp_i, sin_v * amp_r + cos_v * amp_i], axis=2)
    right = jnp.concatenate(
        [jnp.concatenate([cos_v, sin_v], axis=2), jnp.concatenate([-sin_v, cos_v], axis=2)], axis=1
    )
    both = jnp.einsum("kbm,kcm->kbc", left, right, precision=lax.Precision.HIGHEST)
    return both[:, :, :quarter], both[:, :, quarter:]


def pack(real, imag, sign):
    top = jnp.concatenate([real, -sign * imag], axis=2)
    low = jnp.concatenate([sign * imag, real], axis=2)
    return split_high_low(jnp.concatenate([top, low], axis=1))


def column_matrix(real, imag):
    return pack(real, imag, 1.0)


def row_matrix(real, imag):
    turned_r = jnp.stack([real[0], real[3], real[2], real[1]])
    turned_i = jnp.stack([imag[0], imag[3], imag[2], imag[1]])
    return pack(turned_r, turned_i, -1.0)


def butterfly(re, im, sign):
    sum_r, dif_r = re[0] + re[2], re[0] - re[2]
    sum_i, dif_i = im[0] + im[2], im[0] - im[2]
    odd_r, gap_r = re[1] + re[3], re[1] - re[3]
    odd_i, gap_i = im[1] + im[3], im[1] - im[3]
    if sign < 0:
        gap_r, gap_i = -gap_r, -gap_i
    out_r = [sum_r + odd_r, dif_r - gap_i, sum_r - odd_r, dif_r + gap_i]
    out_i = [sum_i + odd_i, dif_i + gap_r, sum_i - odd_i, dif_i - gap_r]
    return out_r, out_i


def halves(value):
    high = value.astype(jnp.bfloat16)
    return high, (value - high.astype(jnp.float32)).astype(jnp.bfloat16)


def dot(left, right):
    return jnp.dot(left, right, preferred_element_type=jnp.float32)


def filter_rows(re, im, high_ref, low_ref):
    quarter = re[0].shape[1]
    re, im = butterfly(re, im, -1)
    out_r, out_i = [], []
    for k in range(4):
        high, low = halves(jnp.concatenate([re[k], im[k]], axis=1))
        out = dot(high, high_ref[k]) + (dot(low, high_ref[k]) + dot(high, low_ref[k]))
        out_r.append(out[:, :quarter])
        out_i.append(out[:, quarter:])
    return butterfly(out_r, out_i, 1)


def filter_cols(re, im, high_ref, low_ref):
    quarter = re[0].shape[0]
    re, im = butterfly(re, im, -1)
    out_r, out_i = [], []
    for k in range(4):
        high, low = halves(jnp.concatenate([re[k], im[k]], axis=0))
        out = dot(high_ref[k], high) + (dot(high_ref[k], low) + dot(low_ref[k], high))
        out_r.append(out[:quarter])
        out_i.append(out[quarter:])
    return butterfly(out_r, out_i, 1)


def first_kernel(sign, field_ref, high_ref, low_ref, out_ref):
    quarter = field_ref.shape[3] // 4
    re, im = [], []
    for j in range(4):
        span = pl.ds(j * quarter, quarter)
        re.append(field_ref[0, 0, :, span])
        im.append(sign * field_ref[1, 0, :, span])
    re, im = filter_rows(re, im, high_ref, low_ref)
    for j in range(4):
        out_ref[j, 0] = re[j]
        out_ref[j, 1] = im[j]


def middle_step(cos_ref, sin_ref, field_ref, high_ref, low_ref, out_ref, keep):
    re = [field_ref[j, 0] for j in range(4)]
    im = [field_ref[j, 1] for j in range(4)]
    re, im = filter_cols(re, im, high_ref, low_ref)
    for j in range(4):
        cos_v, sin_v = cos_ref[j], sin_ref[j]
        re[j], im[j] = re[j] * cos_v - im[j] * sin_v, im[j] * cos_v + re[j] * sin_v
        keep(j, re[j], im[j])
    re, im = filter_cols(re, im, high_ref, low_ref)
    for j in range(4):
        out_ref[j, 0] = re[j]
        out_ref[j, 1] = im[j]


def middle_source(cos_ref, sin_ref, field_ref, high_ref, low_ref, out_ref, mid_ref):
    def keep(j, re, im):
        mid_ref[j, 0] = re
        mid_ref[j, 1] = im

    middle_step(cos_ref, sin_ref, field_ref, high_ref, low_ref, out_ref, keep)


def middle_receiver(cos_ref, sin_ref, field_ref, high_ref, low_ref, mid_ref, out_ref, term_ref):
    def keep(j, re, im):
        term_ref[j] = mid_ref[j, 0] * re - mid_ref[j, 1] * im

    middle_step(cos_ref, sin_ref, field_ref, high_ref, low_ref, out_ref, keep)


def last_step(cos_ref, sin_ref, field_ref, high_ref, low_ref, keep):
    quarter = field_ref.shape[3]
    re = [field_ref[j, 0] for j in range(4)]
    im = [field_ref[j, 1] for j in range(4)]
    re, im = filter_rows(re, im, high_ref, low_ref)
    for j in range(4):
        span = pl.ds(j * quarter, quarter)
        cos_v, sin_v = cos_ref[:, span], sin_ref[:, span]
        keep(span, re[j] * cos_v - im[j] * sin_v, im[j] * cos_v + re[j] * sin_v)


def last_source(cos_ref, sin_ref, field_ref, high_ref, low_ref, source_ref):
    def keep(span, re, im):
        source_ref[0, 0, :, span] = re
        source_ref[1, 0, :, span] = im

    last_step(cos_ref, sin_ref, field_ref, high_ref, low_ref, keep)


def last_receiver(cos_ref, sin_ref, field_ref, high_ref, low_ref, source_ref, receiver_ref, term_ref):
    def keep(span, re, im):
        term_ref[span.start // span.size] = (
            source_ref[0, 0, :, span] * re - source_ref[1, 0, :, span] * im
        )
        receiver_ref[0, 0, :, span] = re
        receiver_ref[1, 0, :, span] = -im

    last_step(cos_ref, sin_ref, field_ref, high_ref, low_ref, keep)


def params():
    return pltpu.CompilerParams(vmem_limit_bytes=vmem_bytes, dimension_semantics=("arbitrary",))


def whole(shape):
    return pl.BlockSpec(shape, lambda i: (0,) * len(shape))


def swap(blocks):
    return lax.all_to_all(blocks, "row", split_axis=0, concat_axis=0, tiled=True)


def sum_strips(strips):
    count = strips.shape[0]
    me = lax.axis_index("freq")
    total = lax.dynamic_index_in_dim(strips, me, 0, keepdims=False)
    for shift in range(1, count):
        sent = lax.dynamic_index_in_dim(strips, (me + shift) % count, 0, keepdims=False)
        total = total + lax.ppermute(sent, "freq", [(i, (i + shift) % count) for i in range(count)])
    return total


def body(source_field, receiver_field, slowness, owner, freq_index):
    rows, width = source_field.shape[2:]
    row_count = lax.axis_size("row")
    freq_count = lax.axis_size("freq")
    height = rows * row_count
    cols = width // row_count
    quart_w = width // 4
    quart_h = height // 4
    more = row_count // 4
    omega = 2.0 * math.pi * (base_hertz + step_hertz * freq_index.astype(jnp.float32))

    def turning(slab):
        theta = slab * (omega[0] * dz_km)
        return jnp.cos(theta), jnp.sin(theta)

    def owned(depth):
        return jnp.where(lax.axis_index("freq") == owner[depth], slowness[0], 0.0)

    turned = swap(jnp.moveaxis(owned(0).reshape(rows, row_count, cols), 1, 0))
    piece_last = lax.psum_scatter(owned(1), "freq", scatter_dimension=0, tiled=True)
    source_field, turned = lax.optimization_barrier((source_field, turned))
    turned, piece_last = lax.optimization_barrier((turned, piece_last))
    piece = lax.psum_scatter(turned, "freq", scatter_dimension=0, tiled=True)
    receiver_field, piece = lax.optimization_barrier((receiver_field, piece))
    slab_first = lax.all_gather(piece, "freq", axis=0, tiled=True)
    piece_last, slab_first = lax.optimization_barrier((piece_last, slab_first))
    slab_last = lax.all_gather(piece_last, "freq", axis=0, tiled=True)
    turn_first = turning(slab_first.reshape(4, quart_h, cols))

    block_w = toeplitz_blocks(width, omega[0])
    block_h = block_w if height == width else toeplitz_blocks(height, omega[0])
    row_high, row_low = row_matrix(*block_w)
    col_high, col_low = column_matrix(*block_h)
    mat_w = whole((4, 2 * quart_w, 2 * quart_w))
    mat_h = whole((4, 2 * quart_h, 2 * quart_h))

    step = min(rows, 128)
    row_block = pl.BlockSpec((2, 1, step, width), lambda i: (0, 0, i, 0))
    quarter_block = pl.BlockSpec((4, 2, step, quart_w), lambda i: (0, 0, i, 0))
    line_block = pl.BlockSpec((step, width), lambda i: (i, 0))
    col_block = pl.BlockSpec((4, 2, quart_h, cols), lambda i: (0, 0, 0, 0))
    term_block = pl.BlockSpec((4, quart_h, cols), lambda i: (0, 0, 0))
    quarter_shape = jax.ShapeDtypeStruct((4, 2, rows, quart_w), jnp.float32)
    col_shape = jax.ShapeDtypeStruct((4, 2, quart_h, cols), jnp.float32)
    term_shape = jax.ShapeDtypeStruct((4, quart_h, cols), jnp.float32)
    strip_block = pl.BlockSpec((4, step, quart_w), lambda i: (0, i, 0))
    strip_shape = jax.ShapeDtypeStruct((4, rows, quart_w), jnp.float32)
    field_shape = jax.ShapeDtypeStruct(source_field.shape, jnp.float32)

    def first(field, sign):
        return pl.pallas_call(
            partial(first_kernel, sign),
            grid=(rows // step,),
            in_specs=[row_block, mat_w, mat_w],
            out_specs=quarter_block,
            out_shape=quarter_shape,
            compiler_params=params(),
        )(field, row_high, row_low)

    def to_cols(fields):
        if more > 1:
            fields = fields.reshape(4, 2, rows, more, cols)
            fields = jnp.moveaxis(fields, 3, 1).reshape(row_count, 2, rows, cols)
        fields = swap(fields)
        if more > 1:
            fields = fields.reshape(4, more, 2, rows, cols)
            fields = jnp.moveaxis(fields, 1, 2).reshape(4, 2, quart_h, cols)
        return fields

    def to_rows(fields):
        if more > 1:
            fields = fields.reshape(4, 2, more, rows, cols)
            fields = jnp.moveaxis(fields, 2, 1).reshape(row_count, 2, rows, cols)
        fields = swap(fields)
        if more > 1:
            fields = fields.reshape(4, more, 2, rows, cols)
            fields = jnp.moveaxis(fields, 1, 3).reshape(4, 2, rows, quart_w)
        return fields

    source = to_cols(first(source_field, 1.0))
    receiver = to_cols(first(receiver_field, -1.0))
    source, middle = pl.pallas_call(
        middle_source,
        grid=(1,),
        in_specs=[term_block, term_block, col_block, mat_h, mat_h],
        out_specs=[col_block, col_block],
        out_shape=[col_shape, col_shape],
        compiler_params=params(),
    )(*turn_first, source, col_high, col_low)
    source = to_rows(source)
    receiver, term = pl.pallas_call(
        middle_receiver,
        grid=(1,),
        in_specs=[term_block, term_block, col_block, mat_h, mat_h, col_block],
        out_specs=[col_block, term_block],
        out_shape=[col_shape, term_shape],
        compiler_params=params(),
    )(*turn_first, receiver, col_high, col_low, middle)
    receiver, term, slab_last = lax.optimization_barrier((receiver, term, slab_last))
    turn_last = turning(slab_last)
    receiver = to_rows(receiver)

    term = term.reshape(height, cols)
    if row_count == freq_count:
        part = lax.psum_scatter(term, "freq", scatter_dimension=0, tiled=True)
        pairs = [
            (r * freq_count + f, f * freq_count + r)
            for r in range(row_count)
            for f in range(freq_count)
        ]
        image_first = lax.ppermute(part, ("row", "freq"), pairs)
    else:
        term = lax.all_to_all(term, "row", split_axis=0, concat_axis=1, tiled=True)
        image_first = lax.psum_scatter(term, "freq", scatter_dimension=1, tiled=True)

    source_out = pl.pallas_call(
        last_source,
        grid=(rows // step,),
        in_specs=[line_block, line_block, quarter_block, mat_w, mat_w],
        out_specs=row_block,
        out_shape=field_shape,
        compiler_params=params(),
    )(*turn_last, source, row_high, row_low)
    receiver_out, term = pl.pallas_call(
        last_receiver,
        grid=(rows // step,),
        in_specs=[line_block, line_block, quarter_block, mat_w, mat_w, row_block],
        out_specs=[row_block, strip_block],
        out_shape=[field_shape, strip_shape],
        compiler_params=params(),
    )(*turn_last, receiver, row_high, row_low, source_out)
    if freq_count == 4:
        image_last = sum_strips(term)
    else:
        term = jnp.moveaxis(term, 0, 1).reshape(rows, width)
        image_last = lax.psum_scatter(term, "freq", scatter_dimension=1, tiled=True)
    return source_out, receiver_out, jnp.stack([image_first, image_last])


fused_vmem = 60 * 1024 * 1024
MESH = pl.DeviceIdType.MESH


def filter_table(length, count):
    quarter = length // 4
    offset = np.arange(2 * quarter)
    offset = np.where(offset < quarter, -offset, 2 * quarter - offset)
    place = np.arange(quarter)
    table = np.zeros((count, 8, 2 * quarter), np.float32)
    kmax = math.pi / dx_km
    for slot in range(count):
        omega = 2.0 * math.pi * (base_hertz + step_hertz * slot)
        for k in range(4):
            kept = 4 * place + k
            signed = np.where(kept * 2 < length, kept, kept - length)
            square = (signed * (2.0 * math.pi / (length * dx_km))) ** 2
            amp = np.exp(-taper * square / kmax**2 - 1j * (dz_km / omega) * square) / length
            turns = (offset[:, None] * kept[None, :]) % length
            kernel = np.exp(2j * math.pi / length * turns) @ amp
            table[slot, k] = kernel.real
            table[slot, 4 + k] = kernel.imag
    return table


def turn_of(theta):
    square = theta * theta
    cos_v = 1.0 / 87178291200.0
    sin_v = 1.0 / 1307674368000.0
    cos_v = 1.0 / 479001600.0 - square * cos_v
    sin_v = 1.0 / 6227020800.0 - square * sin_v
    for even in (10, 8, 6, 4, 2, 0):
        cos_v = 1.0 / math.factorial(even) - square * cos_v
        sin_v = 1.0 / math.factorial(even + 1) - square * sin_v
    return cos_v, theta * sin_v


def row_pass(re, im, mats):
    step, quarter = re[0].shape
    re, im = butterfly(re, im, 1)
    out_r, out_i = [], []
    for k in range(4):
        turned = (4 - k) % 4
        high, low = halves(jnp.concatenate([re[k], im[k]], axis=1))
        out = dot(jnp.concatenate([high, low], axis=0), mats[turned])
        out = out[:step] + (out[step:] + dot(high, mats[4 + turned]))
        out_r.append(out[:, :quarter])
        out_i.append(out[:, quarter:])
    return butterfly(out_r, out_i, -1)


def col_pass(re, im, mats):
    quarter = re[0].shape[0]
    re, im = butterfly(re, im, -1)
    out_r, out_i = [], []
    for k in range(4):
        high, low = halves(jnp.concatenate([re[k], im[k]], axis=0))
        out = dot(mats[k], high) + (dot(mats[k], low) + dot(mats[4 + k], high))
        out_r.append(out[:quarter])
        out_i.append(out[quarter:])
    return butterfly(out_r, out_i, 1)


def wait_for(ref, sem):
    pltpu.make_async_copy(ref, ref, sem).wait()


def fused_kernel(
    step, late_step, tail_step, owner, slot, src_in, rec_in, slow_in, table_in, src_out, rec_out, img_out,
    field, table, mats, slab, early, cols, mid, store, masked, shared, piece, grid_first, grid_last,
    cos_first, sin_first, cos_last, sin_last, term_first, got_first, part_first, term_last, got_last, image,
    load_sem, store_sem, early_send, cols_recv, own_sem, late_send, lines_recv,
    shared_send, shared_recv, piece_send, piece_recv, depth_send, depth_recv, across_send, across_recv,
    first_send, first_recv, cross_send, cross_recv, last_send, last_recv,
):
    shot, row, freq = lax.axis_index("shot"), lax.axis_index("row"), lax.axis_index("freq")
    rows, width = slab.shape
    quarter = width // 4
    half = quarter // 2
    chunks = rows // step
    late_count = rows // late_step
    tail_count = late_step // tail_step
    eighth = rows // 8
    chip, core = lax.div(row, 2), lax.rem(row, 2)
    row_peers = [(1 - chip) * 2 + core, (1 - chip) * 2 + 1 - core, chip * 2 + 1 - core]
    freq_peers = [lax.rem(freq + 1, 4), lax.rem(freq + 3, 4), lax.rem(freq + 2, 4)]

    def send(source, target, send_sem, recv_sem, device):
        pltpu.make_async_remote_copy(
            src_ref=source, dst_ref=target, send_sem=send_sem, recv_sem=recv_sem,
            device_id=device, device_id_type=MESH,
        ).start()

    def span(c, size=step):
        return pl.ds(pl.multiple_of(c * size, size), size)

    def tail_span(c):
        return pl.ds(pl.multiple_of(rows - late_step + c * tail_step, tail_step), tail_step)

    def pieces(values):
        return [
            jnp.concatenate([values[b][:, x * half : (x + 1) * half] for b in (core, core + 2)], axis=1)
            for x in range(2)
            for core in range(2)
        ]

    loads = [
        pltpu.make_async_copy(table_in, table, load_sem.at[1]),
        pltpu.make_async_copy(src_in.at[:, 0], field.at[0], load_sem.at[0]),
        pltpu.make_async_copy(slow_in.at[0], slab, load_sem.at[2]),
        pltpu.make_async_copy(rec_in.at[:, 0], field.at[1], load_sem.at[3]),
    ]
    for load in loads:
        load.start()

    barrier = pltpu.get_barrier_semaphore()
    peers = [(shot, peer, freq) for peer in row_peers] + [(shot, row, peer) for peer in freq_peers]
    for device in peers + [(1 - shot, row, freq)]:
        pl.semaphore_signal(barrier, inc=1, device_id=device, device_id_type=MESH)

    omega_dz = (2.0 * math.pi * dz_km) * (base_hertz + step_hertz * slot[0].astype(jnp.float32))

    def early_rows(which, c):
        place = span(c)
        re = [field[which, 0, place, j * quarter : (j + 1) * quarter] for j in range(4)]
        im = [field[which, 1, place, j * quarter : (j + 1) * quarter] for j in range(4)]
        if which == 0:
            im = [-v for v in im]
        re, im = row_pass(re, im, mats)
        re, im = pieces(re), pieces(im)
        for j in range(4):
            early[which, c, j, 0] = re[j]
            early[which, c, j, 1] = -im[j]

    def early_go(which, c):
        target = cols.at[which, row, :, span(c), :]
        for peer in row_peers:
            send(early.at[which, c, peer], target, early_send.at[which], cols_recv.at[which], (shot, peer, freq))
        pltpu.make_async_copy(early.at[which, c, row], target, own_sem.at[0, which]).start()

    def late_go(which, place, piece_no):
        target = store.at[2 + which, row, :, place, :]
        for peer in row_peers:
            send(
                store.at[which, peer, :, place, :], target,
                late_send.at[which], lines_recv.at[which, piece_no], (shot, peer, freq),
            )

    def share_go(depth):
        for peer in freq_peers:
            send(masked.at[depth, peer], shared.at[depth, freq], shared_send.at[depth], shared_recv.at[depth], (shot, row, peer))

    def share_sum(depth):
        shared[depth, freq] = masked[depth, freq]
        wait_for(shared.at[depth, pl.ds(0, 3)], shared_recv.at[depth])
        return (shared[depth, 0] + shared[depth, 1]) + (shared[depth, 2] + shared[depth, 3])

    def gather_go(depth, ref):
        for peer in freq_peers:
            send(ref.at[shot, freq], ref.at[shot, freq], depth_send.at[depth], depth_recv.at[depth, freq], (shot, row, peer))
        send(ref.at[shot, freq], ref.at[shot, freq], across_send.at[depth], across_recv.at[depth], (1 - shot, row, freq))

    def gather_end(depth, ref):
        for peer in freq_peers:
            block = ref.at[shot, peer]
            wait_for(block, depth_recv.at[depth, peer])
            send(block, block, across_send.at[depth], across_recv.at[depth], (1 - shot, row, freq))

    def gather_wait(depth, ref):
        wait_for(ref.at[1 - shot], across_recv.at[depth])

    loads[0].wait()
    kernels = table[slot[0]]

    def toeplitz(i):
        wide = jnp.broadcast_to(kernels[i : i + 1], (half, 2 * quarter))
        turned_rows = pltpu.roll(wide, 0, 1, stride=1, stride_axis=0)
        return [halves(turned_rows[:, n * half : (n + 1) * half]) for n in (0, 1, 3)]

    for k in range(4):
        reals, imags = toeplitz(k), toeplitz(4 + k)
        for r, c, n in ((0, 0, 0), (0, half, 1), (half, 0, 2), (half, half, 0)):
            near, far = slice(r, r + half), slice(quarter + r, quarter + r + half)
            near_c, far_c = slice(c, c + half), slice(quarter + c, quarter + c + half)
            for at, real, imag in zip((k, 4 + k), reals[n], imags[n]):
                mats[at, near, near_c] = real
                mats[at, far, far_c] = real
                mats[at, far, near_c] = imag
                mats[at, near, far_c] = -imag
    loads[1].wait()
    early_rows(0, 0)
    pl.semaphore_wait(barrier, 7)
    early_go(0, 0)
    loads[2].wait()
    for depth in range(2):
        mine = jnp.where(owner[depth] == freq, 1.0, 0.0)
        for k in range(4):
            base = pl.multiple_of((shot * 4 + k) * eighth, eighth)
            masked[depth, k] = slab[pl.ds(base, eighth), :] * mine
    share_go(0)

    @pl.loop(1, chunks)
    def _(c):
        early_rows(0, c)
        early_go(0, c)

    loads[3].wait()

    @pl.loop(0, chunks)
    def _(c):
        early_rows(1, c)

    total = share_sum(0)
    parts = pieces([total[:, b * quarter : (b + 1) * quarter] for b in range(4)])
    for j in range(4):
        piece[j] = parts[j]
    for peer in row_peers:
        send(piece.at[peer], grid_first.at[shot, freq, row], piece_send, piece_recv, (shot, peer, freq))
    grid_first[shot, freq, row] = piece[row]
    share_go(1)
    for c in range(chunks):
        early_go(1, c)
    wait_for(grid_first.at[shot, freq, pl.ds(0, 3)], piece_recv)
    gather_go(0, grid_first)

    def col_ready(which):
        wait_for(cols.at[which, 0], own_sem.at[0, which])
        wait_for(cols.at[which, pl.ds(0, 3)], cols_recv.at[which])

    def col_first(which):
        return col_pass([cols[which, j, 0] for j in range(4)], [cols[which, j, 1] for j in range(4)], mats)

    def turned(j, re, im):
        return re * cos_first[j] - im * sin_first[j], im * cos_first[j] + re * sin_first[j]

    def col_second(which, re, im):
        re, im = col_pass(re, im, mats)
        for j in range(4):
            store[which, j, 0] = re[j]
            store[which, j, 1] = im[j]
        pltpu.make_async_copy(store.at[which, row], store.at[2 + which, row], own_sem.at[1, which]).start()

    col_ready(0)
    re, im = col_first(0)
    for j in range(4):
        mid[j, 0] = re[j]
        mid[j, 1] = im[j]
    gather_end(0, grid_first)
    grid_last[shot, freq] = share_sum(1)
    gather_go(1, grid_last)
    gather_wait(0, grid_first)
    for j in range(4):
        theta = grid_first[:, :, j].reshape(rows, quarter) * omega_dz
        cos_first[j], sin_first[j] = turn_of(theta)
    re, im = [], []
    for j in range(4):
        real, imag = turned(j, mid[j, 0], mid[j, 1])
        mid[j, 0] = real
        mid[j, 1] = imag
        re.append(real)
        im.append(imag)
    col_second(0, re, im)
    for c in range(2):
        late_go(0, span(c, rows // 2), c)

    col_ready(1)
    re, im = col_first(1)
    for j in range(4):
        re[j], im[j] = turned(j, re[j], im[j])
        term = mid[j, 0] * re[j] - mid[j, 1] * im[j]
        for h in range(2):
            term_first[h, j] = term[:, h * half : (h + 1) * half]
    for h in range(2):
        peer = core + 2 * h

        @pl.when(peer != freq)
        def _(h=h, peer=peer):
            send(term_first.at[h], got_first.at[freq], first_send.at[h], first_recv.at[freq], (shot, row, peer))

    col_second(1, re, im)

    gather_end(1, grid_last)
    gather_wait(1, grid_last)
    cos_last[...], sin_last[...] = turn_of(grid_last[...].reshape(rows, width) * omega_dz)

    def final_rows(which, place, piece_no):
        wait_for(store.at[2 + which, pl.ds(0, 3), :, place, :], lines_recv.at[which, piece_no])

        def gathered(b, part):
            lanes = slice((b // 2) * half, (b // 2 + 1) * half)
            return jnp.concatenate([store[2 + which, 2 * x + b % 2, part, place, lanes] for x in range(2)], axis=1)

        re = [gathered(b, 0) for b in range(4)]
        im = [-gathered(b, 1) for b in range(4)]
        re, im = row_pass(re, im, mats)
        for j in range(4):
            here = slice(j * quarter, (j + 1) * quarter)
            cos_v, sin_v = cos_last[place, here], sin_last[place, here]
            real = re[j] * cos_v + im[j] * sin_v
            imag = im[j] * cos_v - re[j] * sin_v
            if which == 0:
                imag = -imag
            else:
                term_last[j, place, :] = field[0, 0, place, here] * real + field[0, 1, place, here] * imag
            field[which, 0, place, here] = real
            field[which, 1, place, here] = imag
        out = (src_out, rec_out)[which]
        pltpu.make_async_copy(field.at[which, :, place, :], out.at[:, 0, place, :], store_sem.at[which]).start()

    for c in range(late_count - 1):
        late_go(1, span(c, late_step), c)
    for c in range(tail_count):
        late_go(1, tail_span(c), late_count + c)
    wait_for(store.at[0, 0], own_sem.at[1, 0])
    wait_for(store.at[1, 0], own_sem.at[1, 1])

    @pl.loop(0, 2)
    def _(c):
        final_rows(0, span(c, rows // 2), c)

    active = lax.rem(freq, 2) == core
    strip = pl.ds(pl.multiple_of(chip * half, half), half)

    @pl.when(active)
    def _():
        got_first[freq] = term_first[lax.div(freq, 2)]
        for peer in freq_peers:
            wait_for(got_first.at[peer], first_recv.at[peer])
        for a in range(4):
            part_first[a] = (got_first[0, a] + got_first[1, a]) + (got_first[2, a] + got_first[3, a])
        for peer in row_peers:
            send(part_first.at[peer], image.at[0, :, strip], cross_send, cross_recv.at[chip], (shot, peer, freq))
        image[0, :, strip] = part_first[row]

    def last_rows(place, piece_no):
        final_rows(1, place, piece_no)
        for peer in freq_peers:
            send(
                term_last.at[peer, place, :], got_last.at[freq, place, :],
                last_send, last_recv.at[piece_no], (shot, row, peer),
            )

    @pl.loop(0, late_count - 1)
    def _(c):
        last_rows(span(c, late_step), c)

    @pl.loop(0, tail_count)
    def _(c):
        last_rows(tail_span(c), late_count + c)

    got_last[freq] = term_last[freq]
    other = pl.ds(pl.multiple_of((1 - chip) * half, half), half)
    wait_for(image.at[0, :, other], cross_recv.at[1 - chip])

    @pl.when(active)
    def _():
        wait_for(part_first.at[pl.ds(0, 3)], cross_send)

    @pl.when(jnp.logical_not(active))
    def _():
        wait_for(image.at[0, :, strip], cross_recv.at[chip])

    pltpu.make_async_copy(image.at[0], img_out.at[0], store_sem.at[2]).start()

    def last_sum(place, piece_no):
        wait_for(got_last.at[pl.ds(0, 3), place, :], last_recv.at[piece_no])
        image[1, place, :] = (got_last[0, place, :] + got_last[1, place, :]) + (
            got_last[2, place, :] + got_last[3, place, :]
        )

    @pl.loop(0, late_count - 1)
    def _(c):
        last_sum(span(c, late_step), c)

    @pl.loop(0, tail_count)
    def _(c):
        last_sum(tail_span(c), late_count + c)

    pltpu.make_async_copy(image.at[1], img_out.at[1], store_sem.at[3]).start()

    wait_for(piece.at[pl.ds(0, 3)], piece_send)
    for depth, ref in enumerate((grid_first, grid_last)):
        wait_for(masked.at[depth, pl.ds(0, 3)], shared_send.at[depth])
        wait_for(ref.at[0, pl.ds(0, 3)], depth_send.at[depth])
        wait_for(ref.at[0], across_send.at[depth])
    for which in range(2):
        wait_for(early.at[which, :, pl.ds(0, 3)], early_send.at[which])
        wait_for(store.at[which, pl.ds(0, 3)], late_send.at[which])
    for h in range(2):

        @pl.when(core + 2 * h != freq)
        def _(h=h):
            wait_for(term_first.at[h], first_send.at[h])

    wait_for(term_last.at[pl.ds(0, 3)], last_send)
    wait_for(field.at[0], store_sem.at[0])
    wait_for(field.at[1], store_sem.at[1])
    wait_for(image.at[0], store_sem.at[2])
    wait_for(image.at[1], store_sem.at[3])


def copy_kernel(count, *refs):
    places, outs, holds = refs[:count], refs[count : 2 * count], refs[2 * count : 3 * count]
    load_sem, store_sem = refs[3 * count :]
    loads = [pltpu.make_async_copy(places[i], holds[i], load_sem.at[i]) for i in range(count)]
    stores = [pltpu.make_async_copy(holds[i], outs[i], store_sem.at[i]) for i in range(count)]
    for load in loads:
        load.start()
    for load, store in zip(loads, stores):
        load.wait()
        store.start()
    for store in stores:
        store.wait()


def copied(arrays):
    any_spec = pl.BlockSpec(memory_space=pl.ANY)
    count = len(arrays)
    return pl.pallas_call(
        partial(copy_kernel, count),
        out_shape=[jax.ShapeDtypeStruct(a.shape, a.dtype) for a in arrays],
        in_specs=[any_spec] * count,
        out_specs=[any_spec] * count,
        scratch_shapes=[pltpu.VMEM(a.shape, a.dtype) for a in arrays] + [pltpu.SemaphoreType.DMA((count,))] * 2,
        compiler_params=pltpu.CompilerParams(vmem_limit_bytes=fused_vmem),
    )(*arrays)


def fused_body(table, source_field, receiver_field, slowness, owner, freq_index):
    rows, width = source_field.shape[2:]
    quarter = width // 4
    chunks = 8
    step = rows // chunks
    late_step = rows // 8
    tail_step = late_step // 1

    def floats(*shape):
        return pltpu.VMEM(shape, jnp.float32)

    dma = pltpu.SemaphoreType.DMA
    block = (4, 2, rows, quarter)
    small = pl.BlockSpec(memory_space=pltpu.SMEM)
    any_spec = pl.BlockSpec(memory_space=pl.ANY)
    outs = pl.pallas_call(
        partial(fused_kernel, step, late_step, tail_step),
        out_shape=[
            jax.ShapeDtypeStruct(source_field.shape, jnp.float32),
            jax.ShapeDtypeStruct(source_field.shape, jnp.float32),
            jax.ShapeDtypeStruct((2, rows, quarter), jnp.float32),
        ],
        in_specs=[small] * 2 + [any_spec] * 4,
        out_specs=[any_spec] * 3,
        scratch_shapes=[
            floats(2, 2, rows, width),
            floats(*table.shape),
            pltpu.VMEM((8, 2 * quarter, 2 * quarter), jnp.bfloat16),
            floats(rows, width),
            floats(2, chunks, 4, 2, step, quarter),
            floats(2, *block),
            floats(*block),
            floats(4, *block),
            floats(2, 4, rows // 8, width),
            floats(2, 4, rows // 8, width),
            floats(4, rows // 8, quarter),
            floats(2, 4, 4, rows // 8, quarter),
            floats(2, 4, rows // 8, width),
            floats(4, rows, quarter),
            floats(4, rows, quarter),
            floats(rows, width),
            floats(rows, width),
            floats(2, 4, rows, quarter // 2),
            floats(4, 4, rows, quarter // 2),
            floats(4, rows, quarter // 2),
            floats(4, rows, quarter),
            floats(4, rows, quarter),
            floats(2, rows, quarter),
            dma((6,)), dma((4,)), dma((2,)), dma((2,)), dma((2, 2)), dma((2,)), dma((2, 16)),
            dma((2,)), dma((2,)), dma, dma, dma((2,)), dma((2, 4)), dma((2,)), dma((2,)),
            dma((2,)), dma((4,)), dma, dma((2,)), dma, dma((16,)),
        ],
        compiler_params=pltpu.CompilerParams(
            collective_id=0, has_side_effects=True, vmem_limit_bytes=fused_vmem
        ),
    )(owner, freq_index, source_field, receiver_field, slowness, table)
    return tuple(copied(outs))


def solution(mesh):
    in_specs = (
        P(None, ("shot", "freq"), "row", None),
        P(None, ("shot", "freq"), "row", None),
        P("freq", "row", None),
        P(),
        P(("shot", "freq")),
    )
    out_specs = (
        P(None, ("shot", "freq"), "row", None),
        P(None, ("shot", "freq"), "row", None),
        P("shot", "row", "freq"),
    )
    sizes = tuple(mesh.shape[name] for name in ("shot", "row", "freq"))

    def whole_program(source_field, *rest):
        height, width = source_field.shape[2:]
        part = body
        if sizes == (2, 4, 4) and height == width and width % 1024 == 0:
            part = partial(fused_body, filter_table(width, sizes[2]))
        return jax.shard_map(part, mesh=mesh, in_specs=in_specs, out_specs=out_specs, check_vma=False)(
            source_field, *rest
        )

    return whole_program
```

```python
import math
from functools import partial

import jax
import jax.numpy as jnp
import numpy as np
from jax import lax
from jax.experimental import pallas as pl
from jax.experimental.pallas import tpu as pltpu
from jax.sharding import PartitionSpec as P

dz_km = 0.01
dx_km = 0.0125
base_hertz = 3.0
step_hertz = 4.0
taper = 0.5
vmem_bytes = 56 * 1024 * 1024


def split_high_low(value):
    high = lax.reduce_precision(value, 8, 7)
    return high.astype(jnp.bfloat16), (value - high).astype(jnp.bfloat16)


def toeplitz_blocks(length, omega):
    quarter = length // 4
    place = jnp.arange(quarter, dtype=jnp.int32)
    kept = 4 * place[None, :] + jnp.arange(4, dtype=jnp.int32)[:, None]
    signed = jnp.where(kept * 2 < length, kept, kept - length)
    square = (signed.astype(jnp.float32) * (2.0 * math.pi / (length * dx_km))) ** 2
    kmax = math.pi / dx_km
    damp = jnp.exp(-taper * square / (kmax * kmax)) / float(length)
    phase = (-dz_km / omega) * square
    amp_r = (damp * jnp.cos(phase))[:, None, :]
    amp_i = (damp * jnp.sin(phase))[:, None, :]
    turns = (kept[:, None, :] * place[None, :, None] % length).astype(jnp.float32)
    turns = turns * (2.0 * math.pi / length)
    cos_v = jnp.cos(turns)
    sin_v = jnp.sin(turns)
    left = jnp.concatenate([cos_v * amp_r - sin_v * amp_i, sin_v * amp_r + cos_v * amp_i], axis=2)
    right = jnp.concatenate(
        [jnp.concatenate([cos_v, sin_v], axis=2), jnp.concatenate([-sin_v, cos_v], axis=2)], axis=1
    )
    both = jnp.einsum("kbm,kcm->kbc", left, right, precision=lax.Precision.HIGHEST)
    return both[:, :, :quarter], both[:, :, quarter:]


def pack(real, imag, sign):
    top = jnp.concatenate([real, -sign * imag], axis=2)
    low = jnp.concatenate([sign * imag, real], axis=2)
    return split_high_low(jnp.concatenate([top, low], axis=1))


def column_matrix(real, imag):
    return pack(real, imag, 1.0)


def row_matrix(real, imag):
    turned_r = jnp.stack([real[0], real[3], real[2], real[1]])
    turned_i = jnp.stack([imag[0], imag[3], imag[2], imag[1]])
    return pack(turned_r, turned_i, -1.0)


def butterfly(re, im, sign):
    sum_r, dif_r = re[0] + re[2], re[0] - re[2]
    sum_i, dif_i = im[0] + im[2], im[0] - im[2]
    odd_r, gap_r = re[1] + re[3], re[1] - re[3]
    odd_i, gap_i = im[1] + im[3], im[1] - im[3]
    if sign < 0:
        gap_r, gap_i = -gap_r, -gap_i
    out_r = [sum_r + odd_r, dif_r - gap_i, sum_r - odd_r, dif_r + gap_i]
    out_i = [sum_i + odd_i, dif_i + gap_r, sum_i - odd_i, dif_i - gap_r]
    return out_r, out_i


def halves(value):
    high = value.astype(jnp.bfloat16)
    return high, (value - high.astype(jnp.float32)).astype(jnp.bfloat16)


def dot(left, right):
    return jnp.dot(left, right, preferred_element_type=jnp.float32)


def filter_rows(re, im, high_ref, low_ref):
    quarter = re[0].shape[1]
    re, im = butterfly(re, im, -1)
    out_r, out_i = [], []
    for k in range(4):
        high, low = halves(jnp.concatenate([re[k], im[k]], axis=1))
        out = dot(high, high_ref[k]) + (dot(low, high_ref[k]) + dot(high, low_ref[k]))
        out_r.append(out[:, :quarter])
        out_i.append(out[:, quarter:])
    return butterfly(out_r, out_i, 1)


def filter_cols(re, im, high_ref, low_ref):
    quarter = re[0].shape[0]
    re, im = butterfly(re, im, -1)
    out_r, out_i = [], []
    for k in range(4):
        high, low = halves(jnp.concatenate([re[k], im[k]], axis=0))
        out = dot(high_ref[k], high) + (dot(high_ref[k], low) + dot(low_ref[k], high))
        out_r.append(out[:quarter])
        out_i.append(out[quarter:])
    return butterfly(out_r, out_i, 1)


def first_kernel(sign, field_ref, high_ref, low_ref, out_ref):
    quarter = field_ref.shape[3] // 4
    re, im = [], []
    for j in range(4):
        span = pl.ds(j * quarter, quarter)
        re.append(field_ref[0, 0, :, span])
        im.append(sign * field_ref[1, 0, :, span])
    re, im = filter_rows(re, im, high_ref, low_ref)
    for j in range(4):
        out_ref[j, 0] = re[j]
        out_ref[j, 1] = im[j]


def middle_step(cos_ref, sin_ref, field_ref, high_ref, low_ref, out_ref, keep):
    re = [field_ref[j, 0] for j in range(4)]
    im = [field_ref[j, 1] for j in range(4)]
    re, im = filter_cols(re, im, high_ref, low_ref)
    for j in range(4):
        cos_v, sin_v = cos_ref[j], sin_ref[j]
        re[j], im[j] = re[j] * cos_v - im[j] * sin_v, im[j] * cos_v + re[j] * sin_v
        keep(j, re[j], im[j])
    re, im = filter_cols(re, im, high_ref, low_ref)
    for j in range(4):
        out_ref[j, 0] = re[j]
        out_ref[j, 1] = im[j]


def middle_source(cos_ref, sin_ref, field_ref, high_ref, low_ref, out_ref, mid_ref):
    def keep(j, re, im):
        mid_ref[j, 0] = re
        mid_ref[j, 1] = im

    middle_step(cos_ref, sin_ref, field_ref, high_ref, low_ref, out_ref, keep)


def middle_receiver(cos_ref, sin_ref, field_ref, high_ref, low_ref, mid_ref, out_ref, term_ref):
    def keep(j, re, im):
        term_ref[j] = mid_ref[j, 0] * re - mid_ref[j, 1] * im

    middle_step(cos_ref, sin_ref, field_ref, high_ref, low_ref, out_ref, keep)


def last_step(cos_ref, sin_ref, field_ref, high_ref, low_ref, keep):
    quarter = field_ref.shape[3]
    re = [field_ref[j, 0] for j in range(4)]
    im = [field_ref[j, 1] for j in range(4)]
    re, im = filter_rows(re, im, high_ref, low_ref)
    for j in range(4):
        span = pl.ds(j * quarter, quarter)
        cos_v, sin_v = cos_ref[:, span], sin_ref[:, span]
        keep(span, re[j] * cos_v - im[j] * sin_v, im[j] * cos_v + re[j] * sin_v)


def last_source(cos_ref, sin_ref, field_ref, high_ref, low_ref, source_ref):
    def keep(span, re, im):
        source_ref[0, 0, :, span] = re
        source_ref[1, 0, :, span] = im

    last_step(cos_ref, sin_ref, field_ref, high_ref, low_ref, keep)


def last_receiver(cos_ref, sin_ref, field_ref, high_ref, low_ref, source_ref, receiver_ref, term_ref):
    def keep(span, re, im):
        term_ref[span.start // span.size] = (
            source_ref[0, 0, :, span] * re - source_ref[1, 0, :, span] * im
        )
        receiver_ref[0, 0, :, span] = re
        receiver_ref[1, 0, :, span] = -im

    last_step(cos_ref, sin_ref, field_ref, high_ref, low_ref, keep)


def params():
    return pltpu.CompilerParams(vmem_limit_bytes=vmem_bytes, dimension_semantics=("arbitrary",))


def whole(shape):
    return pl.BlockSpec(shape, lambda i: (0,) * len(shape))


def swap(blocks):
    return lax.all_to_all(blocks, "row", split_axis=0, concat_axis=0, tiled=True)


def sum_strips(strips):
    count = strips.shape[0]
    me = lax.axis_index("freq")
    total = lax.dynamic_index_in_dim(strips, me, 0, keepdims=False)
    for shift in range(1, count):
        sent = lax.dynamic_index_in_dim(strips, (me + shift) % count, 0, keepdims=False)
        total = total + lax.ppermute(sent, "freq", [(i, (i + shift) % count) for i in range(count)])
    return total


def body(source_field, receiver_field, slowness, owner, freq_index):
    rows, width = source_field.shape[2:]
    row_count = lax.axis_size("row")
    freq_count = lax.axis_size("freq")
    height = rows * row_count
    cols = width // row_count
    quart_w = width // 4
    quart_h = height // 4
    more = row_count // 4
    omega = 2.0 * math.pi * (base_hertz + step_hertz * freq_index.astype(jnp.float32))

    def turning(slab):
        theta = slab * (omega[0] * dz_km)
        return jnp.cos(theta), jnp.sin(theta)

    def owned(depth):
        return jnp.where(lax.axis_index("freq") == owner[depth], slowness[0], 0.0)

    turned = swap(jnp.moveaxis(owned(0).reshape(rows, row_count, cols), 1, 0))
    piece_last = lax.psum_scatter(owned(1), "freq", scatter_dimension=0, tiled=True)
    source_field, turned = lax.optimization_barrier((source_field, turned))
    turned, piece_last = lax.optimization_barrier((turned, piece_last))
    piece = lax.psum_scatter(turned, "freq", scatter_dimension=0, tiled=True)
    receiver_field, piece = lax.optimization_barrier((receiver_field, piece))
    slab_first = lax.all_gather(piece, "freq", axis=0, tiled=True)
    piece_last, slab_first = lax.optimization_barrier((piece_last, slab_first))
    slab_last = lax.all_gather(piece_last, "freq", axis=0, tiled=True)
    turn_first = turning(slab_first.reshape(4, quart_h, cols))

    block_w = toeplitz_blocks(width, omega[0])
    block_h = block_w if height == width else toeplitz_blocks(height, omega[0])
    row_high, row_low = row_matrix(*block_w)
    col_high, col_low = column_matrix(*block_h)
    mat_w = whole((4, 2 * quart_w, 2 * quart_w))
    mat_h = whole((4, 2 * quart_h, 2 * quart_h))

    step = min(rows, 128)
    row_block = pl.BlockSpec((2, 1, step, width), lambda i: (0, 0, i, 0))
    quarter_block = pl.BlockSpec((4, 2, step, quart_w), lambda i: (0, 0, i, 0))
    line_block = pl.BlockSpec((step, width), lambda i: (i, 0))
    col_block = pl.BlockSpec((4, 2, quart_h, cols), lambda i: (0, 0, 0, 0))
    term_block = pl.BlockSpec((4, quart_h, cols), lambda i: (0, 0, 0))
    quarter_shape = jax.ShapeDtypeStruct((4, 2, rows, quart_w), jnp.float32)
    col_shape = jax.ShapeDtypeStruct((4, 2, quart_h, cols), jnp.float32)
    term_shape = jax.ShapeDtypeStruct((4, quart_h, cols), jnp.float32)
    strip_block = pl.BlockSpec((4, step, quart_w), lambda i: (0, i, 0))
    strip_shape = jax.ShapeDtypeStruct((4, rows, quart_w), jnp.float32)
    field_shape = jax.ShapeDtypeStruct(source_field.shape, jnp.float32)

    def first(field, sign):
        return pl.pallas_call(
            partial(first_kernel, sign),
            grid=(rows // step,),
            in_specs=[row_block, mat_w, mat_w],
            out_specs=quarter_block,
            out_shape=quarter_shape,
            compiler_params=params(),
        )(field, row_high, row_low)

    def to_cols(fields):
        if more > 1:
            fields = fields.reshape(4, 2, rows, more, cols)
            fields = jnp.moveaxis(fields, 3, 1).reshape(row_count, 2, rows, cols)
        fields = swap(fields)
        if more > 1:
            fields = fields.reshape(4, more, 2, rows, cols)
            fields = jnp.moveaxis(fields, 1, 2).reshape(4, 2, quart_h, cols)
        return fields

    def to_rows(fields):
        if more > 1:
            fields = fields.reshape(4, 2, more, rows, cols)
            fields = jnp.moveaxis(fields, 2, 1).reshape(row_count, 2, rows, cols)
        fields = swap(fields)
        if more > 1:
            fields = fields.reshape(4, more, 2, rows, cols)
            fields = jnp.moveaxis(fields, 1, 3).reshape(4, 2, rows, quart_w)
        return fields

    source = to_cols(first(source_field, 1.0))
    receiver = to_cols(first(receiver_field, -1.0))
    source, middle = pl.pallas_call(
        middle_source,
        grid=(1,),
        in_specs=[term_block, term_block, col_block, mat_h, mat_h],
        out_specs=[col_block, col_block],
        out_shape=[col_shape, col_shape],
        compiler_params=params(),
    )(*turn_first, source, col_high, col_low)
    source = to_rows(source)
    receiver, term = pl.pallas_call(
        middle_receiver,
        grid=(1,),
        in_specs=[term_block, term_block, col_block, mat_h, mat_h, col_block],
        out_specs=[col_block, term_block],
        out_shape=[col_shape, term_shape],
        compiler_params=params(),
    )(*turn_first, receiver, col_high, col_low, middle)
    receiver, term, slab_last = lax.optimization_barrier((receiver, term, slab_last))
    turn_last = turning(slab_last)
    receiver = to_rows(receiver)

    term = term.reshape(height, cols)
    if row_count == freq_count:
        part = lax.psum_scatter(term, "freq", scatter_dimension=0, tiled=True)
        pairs = [
            (r * freq_count + f, f * freq_count + r)
            for r in range(row_count)
            for f in range(freq_count)
        ]
        image_first = lax.ppermute(part, ("row", "freq"), pairs)
    else:
        term = lax.all_to_all(term, "row", split_axis=0, concat_axis=1, tiled=True)
        image_first = lax.psum_scatter(term, "freq", scatter_dimension=1, tiled=True)

    source_out = pl.pallas_call(
        last_source,
        grid=(rows // step,),
        in_specs=[line_block, line_block, quarter_block, mat_w, mat_w],
        out_specs=row_block,
        out_shape=field_shape,
        compiler_params=params(),
    )(*turn_last, source, row_high, row_low)
    receiver_out, term = pl.pallas_call(
        last_receiver,
        grid=(rows // step,),
        in_specs=[line_block, line_block, quarter_block, mat_w, mat_w, row_block],
        out_specs=[row_block, strip_block],
        out_shape=[field_shape, strip_shape],
        compiler_params=params(),
    )(*turn_last, receiver, row_high, row_low, source_out)
    if freq_count == 4:
        image_last = sum_strips(term)
    else:
        term = jnp.moveaxis(term, 0, 1).reshape(rows, width)
        image_last = lax.psum_scatter(term, "freq", scatter_dimension=1, tiled=True)
    return source_out, receiver_out, jnp.stack([image_first, image_last])


fused_vmem = 60 * 1024 * 1024
MESH = pl.DeviceIdType.MESH


def filter_table(length, count):
    quarter = length // 4
    offset = np.arange(2 * quarter)
    offset = np.where(offset < quarter, -offset, 2 * quarter - offset)
    place = np.arange(quarter)
    table = np.zeros((count, 8, 2 * quarter), np.float32)
    kmax = math.pi / dx_km
    for slot in range(count):
        omega = 2.0 * math.pi * (base_hertz + step_hertz * slot)
        for k in range(4):
            kept = 4 * place + k
            signed = np.where(kept * 2 < length, kept, kept - length)
            square = (signed * (2.0 * math.pi / (length * dx_km))) ** 2
            amp = np.exp(-taper * square / kmax**2 - 1j * (dz_km / omega) * square) / length
            turns = (offset[:, None] * kept[None, :]) % length
            kernel = np.exp(2j * math.pi / length * turns) @ amp
            table[slot, k] = kernel.real
            table[slot, 4 + k] = kernel.imag
    return table


def turn_of(theta):
    square = theta * theta
    cos_v = 1.0 / 87178291200.0
    sin_v = 1.0 / 1307674368000.0
    cos_v = 1.0 / 479001600.0 - square * cos_v
    sin_v = 1.0 / 6227020800.0 - square * sin_v
    for even in (10, 8, 6, 4, 2, 0):
        cos_v = 1.0 / math.factorial(even) - square * cos_v
        sin_v = 1.0 / math.factorial(even + 1) - square * sin_v
    return cos_v, theta * sin_v


def row_pass(re, im, mats):
    step, quarter = re[0].shape
    re, im = butterfly(re, im, 1)
    out_r, out_i = [], []
    for k in range(4):
        turned = (4 - k) % 4
        high, low = halves(jnp.concatenate([re[k], im[k]], axis=1))
        out = dot(jnp.concatenate([high, low], axis=0), mats[turned])
        out = out[:step] + (out[step:] + dot(high, mats[4 + turned]))
        out_r.append(out[:, :quarter])
        out_i.append(out[:, quarter:])
    return butterfly(out_r, out_i, -1)


def col_pass(re, im, mats):
    quarter = re[0].shape[0]
    re, im = butterfly(re, im, -1)
    out_r, out_i = [], []
    for k in range(4):
        high, low = halves(jnp.concatenate([re[k], im[k]], axis=0))
        out = dot(mats[k], high) + (dot(mats[k], low) + dot(mats[4 + k], high))
        out_r.append(out[:quarter])
        out_i.append(out[quarter:])
    return butterfly(out_r, out_i, 1)


def wait_for(ref, sem):
    pltpu.make_async_copy(ref, ref, sem).wait()


def fused_kernel(
    step, late_step, tail_step, owner, slot, src_in, rec_in, slow_in, table_in, src_out, rec_out, img_out,
    field, table, mats, slab, early, cols, mid, store, masked, shared, piece, grid_first, grid_last,
    cos_first, sin_first, cos_last, sin_last, term_first, got_first, part_first, term_last, got_last, image,
    load_sem, store_sem, early_send, cols_recv, own_sem, late_send, lines_recv,
    shared_send, shared_recv, piece_send, piece_recv, depth_send, depth_recv, across_send, across_recv,
    first_send, first_recv, cross_send, cross_recv, last_send, last_recv,
):
    shot, row, freq = lax.axis_index("shot"), lax.axis_index("row"), lax.axis_index("freq")
    rows, width = slab.shape
    quarter = width // 4
    half = quarter // 2
    chunks = rows // step
    late_count = rows // late_step
    tail_count = late_step // tail_step
    eighth = rows // 8
    chip, core = lax.div(row, 2), lax.rem(row, 2)
    row_peers = [(1 - chip) * 2 + core, (1 - chip) * 2 + 1 - core, chip * 2 + 1 - core]
    freq_peers = [lax.rem(freq + 1, 4), lax.rem(freq + 3, 4), lax.rem(freq + 2, 4)]

    def send(source, target, send_sem, recv_sem, device):
        pltpu.make_async_remote_copy(
            src_ref=source, dst_ref=target, send_sem=send_sem, recv_sem=recv_sem,
            device_id=device, device_id_type=MESH,
        ).start()

    def span(c, size=step):
        return pl.ds(pl.multiple_of(c * size, size), size)

    def tail_span(c):
        return pl.ds(pl.multiple_of(rows - late_step + c * tail_step, tail_step), tail_step)

    def pieces(values):
        return [
            jnp.concatenate([values[b][:, x * half : (x + 1) * half] for b in (core, core + 2)], axis=1)
            for x in range(2)
            for core in range(2)
        ]

    loads = [
        pltpu.make_async_copy(table_in, table, load_sem.at[1]),
        pltpu.make_async_copy(src_in.at[:, 0], field.at[0], load_sem.at[0]),
        pltpu.make_async_copy(slow_in.at[0], slab, load_sem.at[2]),
        pltpu.make_async_copy(rec_in.at[:, 0], field.at[1], load_sem.at[3]),
    ]
    for load in loads:
        load.start()

    barrier = pltpu.get_barrier_semaphore()
    peers = [(shot, peer, freq) for peer in row_peers] + [(shot, row, peer) for peer in freq_peers]
    for device in peers + [(1 - shot, row, freq)]:
        pl.semaphore_signal(barrier, inc=1, device_id=device, device_id_type=MESH)

    omega_dz = (2.0 * math.pi * dz_km) * (base_hertz + step_hertz * slot[0].astype(jnp.float32))

    def early_rows(which, c):
        place = span(c)
        re = [field[which, 0, place, j * quarter : (j + 1) * quarter] for j in range(4)]
        im = [field[which, 1, place, j * quarter : (j + 1) * quarter] for j in range(4)]
        if which == 0:
            im = [-v for v in im]
        re, im = row_pass(re, im, mats)
        re, im = pieces(re), pieces(im)
        for j in range(4):
            early[which, c, j, 0] = re[j]
            early[which, c, j, 1] = -im[j]

    def early_go(which, c):
        target = cols.at[which, row, :, span(c), :]
        for peer in row_peers:
            send(early.at[which, c, peer], target, early_send.at[which], cols_recv.at[which], (shot, peer, freq))
        pltpu.make_async_copy(early.at[which, c, row], target, own_sem.at[0, which]).start()

    def late_go(which, place, piece_no):
        target = store.at[2 + which, row, :, place, :]
        for peer in row_peers:
            send(
                store.at[which, peer, :, place, :], target,
                late_send.at[which], lines_recv.at[which, piece_no], (shot, peer, freq),
            )

    def share_go(depth):
        for peer in freq_peers:
            send(masked.at[depth, peer], shared.at[depth, freq], shared_send.at[depth], shared_recv.at[depth], (shot, row, peer))

    def share_sum(depth):
        shared[depth, freq] = masked[depth, freq]
        wait_for(shared.at[depth, pl.ds(0, 3)], shared_recv.at[depth])
        return (shared[depth, 0] + shared[depth, 1]) + (shared[depth, 2] + shared[depth, 3])

    def gather_go(depth, ref):
        for peer in freq_peers:
            send(ref.at[shot, freq], ref.at[shot, freq], depth_send.at[depth], depth_recv.at[depth, freq], (shot, row, peer))
        send(ref.at[shot, freq], ref.at[shot, freq], across_send.at[depth], across_recv.at[depth], (1 - shot, row, freq))

    def gather_end(depth, ref):
        for peer in freq_peers:
            block = ref.at[shot, peer]
            wait_for(block, depth_recv.at[depth, peer])
            send(block, block, across_send.at[depth], across_recv.at[depth], (1 - shot, row, freq))

    def gather_wait(depth, ref):
        wait_for(ref.at[1 - shot], across_recv.at[depth])

    loads[0].wait()
    kernels = table[slot[0]]

    def toeplitz(i):
        wide = jnp.broadcast_to(kernels[i : i + 1], (half, 2 * quarter))
        turned_rows = pltpu.roll(wide, 0, 1, stride=1, stride_axis=0)
        return [halves(turned_rows[:, n * half : (n + 1) * half]) for n in (0, 1, 3)]

    for k in range(4):
        reals, imags = toeplitz(k), toeplitz(4 + k)
        for r, c, n in ((0, 0, 0), (0, half, 1), (half, 0, 2), (half, half, 0)):
            near, far = slice(r, r + half), slice(quarter + r, quarter + r + half)
            near_c, far_c = slice(c, c + half), slice(quarter + c, quarter + c + half)
            for at, real, imag in zip((k, 4 + k), reals[n], imags[n]):
                mats[at, near, near_c] = real
                mats[at, far, far_c] = real
                mats[at, far, near_c] = imag
                mats[at, near, far_c] = -imag
    loads[1].wait()
    early_rows(0, 0)
    pl.semaphore_wait(barrier, 7)
    early_go(0, 0)
    loads[2].wait()
    for depth in range(2):
        mine = jnp.where(owner[depth] == freq, 1.0, 0.0)
        for k in range(4):
            base = pl.multiple_of((shot * 4 + k) * eighth, eighth)
            masked[depth, k] = slab[pl.ds(base, eighth), :] * mine
    share_go(0)

    @pl.loop(1, chunks)
    def _(c):
        early_rows(0, c)
        early_go(0, c)

    loads[3].wait()

    @pl.loop(0, chunks)
    def _(c):
        early_rows(1, c)

    total = share_sum(0)
    parts = pieces([total[:, b * quarter : (b + 1) * quarter] for b in range(4)])
    for j in range(4):
        piece[j] = parts[j]
    for peer in row_peers:
        send(piece.at[peer], grid_first.at[shot, freq, row], piece_send, piece_recv, (shot, peer, freq))
    grid_first[shot, freq, row] = piece[row]
    share_go(1)
    for c in range(chunks):
        early_go(1, c)
    wait_for(grid_first.at[shot, freq, pl.ds(0, 3)], piece_recv)
    gather_go(0, grid_first)

    def col_ready(which):
        wait_for(cols.at[which, 0], own_sem.at[0, which])
        wait_for(cols.at[which, pl.ds(0, 3)], cols_recv.at[which])

    def col_first(which):
        return col_pass([cols[which, j, 0] for j in range(4)], [cols[which, j, 1] for j in range(4)], mats)

    def turned(j, re, im):
        return re * cos_first[j] - im * sin_first[j], im * cos_first[j] + re * sin_first[j]

    def col_second(which, re, im):
        re, im = col_pass(re, im, mats)
        for j in range(4):
            store[which, j, 0] = re[j]
            store[which, j, 1] = im[j]
        pltpu.make_async_copy(store.at[which, row], store.at[2 + which, row], own_sem.at[1, which]).start()

    col_ready(0)
    re, im = col_first(0)
    for j in range(4):
        mid[j, 0] = re[j]
        mid[j, 1] = im[j]
    gather_end(0, grid_first)
    grid_last[shot, freq] = share_sum(1)
    gather_go(1, grid_last)
    gather_wait(0, grid_first)
    for j in range(4):
        theta = grid_first[:, :, j].reshape(rows, quarter) * omega_dz
        cos_first[j], sin_first[j] = turn_of(theta)
    re, im = [], []
    for j in range(4):
        real, imag = turned(j, mid[j, 0], mid[j, 1])
        mid[j, 0] = real
        mid[j, 1] = imag
        re.append(real)
        im.append(imag)
    col_second(0, re, im)
    for c in range(2):
        late_go(0, span(c, rows // 2), c)

    col_ready(1)
    re, im = col_first(1)
    for j in range(4):
        re[j], im[j] = turned(j, re[j], im[j])
        term = mid[j, 0] * re[j] - mid[j, 1] * im[j]
        for h in range(2):
            term_first[h, j] = term[:, h * half : (h + 1) * half]
    for h in range(2):
        peer = core + 2 * h

        @pl.when(peer != freq)
        def _(h=h, peer=peer):
            send(term_first.at[h], got_first.at[freq], first_send.at[h], first_recv.at[freq], (shot, row, peer))

    col_second(1, re, im)

    gather_end(1, grid_last)
    gather_wait(1, grid_last)
    cos_last[...], sin_last[...] = turn_of(grid_last[...].reshape(rows, width) * omega_dz)

    def final_rows(which, place, piece_no):
        wait_for(store.at[2 + which, pl.ds(0, 3), :, place, :], lines_recv.at[which, piece_no])

        def gathered(b, part):
            lanes = slice((b // 2) * half, (b // 2 + 1) * half)
            return jnp.concatenate([store[2 + which, 2 * x + b % 2, part, place, lanes] for x in range(2)], axis=1)

        re = [gathered(b, 0) for b in range(4)]
        im = [-gathered(b, 1) for b in range(4)]
        re, im = row_pass(re, im, mats)
        for j in range(4):
            here = slice(j * quarter, (j + 1) * quarter)
            cos_v, sin_v = cos_last[place, here], sin_last[place, here]
            real = re[j] * cos_v + im[j] * sin_v
            imag = im[j] * cos_v - re[j] * sin_v
            if which == 0:
                imag = -imag
            else:
                term_last[j, place, :] = field[0, 0, place, here] * real + field[0, 1, place, here] * imag
            field[which, 0, place, here] = real
            field[which, 1, place, here] = imag
        out = (src_out, rec_out)[which]
        pltpu.make_async_copy(field.at[which, :, place, :], out.at[:, 0, place, :], store_sem.at[which]).start()

    for c in range(late_count - 1):
        late_go(1, span(c, late_step), c)
    for c in range(tail_count):
        late_go(1, tail_span(c), late_count + c)
    wait_for(store.at[0, 0], own_sem.at[1, 0])
    wait_for(store.at[1, 0], own_sem.at[1, 1])

    @pl.loop(0, 2)
    def _(c):
        final_rows(0, span(c, rows // 2), c)

    active = lax.rem(freq, 2) == core
    strip = pl.ds(pl.multiple_of(chip * half, half), half)

    @pl.when(active)
    def _():
        got_first[freq] = term_first[lax.div(freq, 2)]
        for peer in freq_peers:
            wait_for(got_first.at[peer], first_recv.at[peer])
        for a in range(4):
            part_first[a] = (got_first[0, a] + got_first[1, a]) + (got_first[2, a] + got_first[3, a])
        for peer in row_peers:
            send(part_first.at[peer], image.at[0, :, strip], cross_send, cross_recv.at[chip], (shot, peer, freq))
        image[0, :, strip] = part_first[row]

    def last_rows(place, piece_no):
        final_rows(1, place, piece_no)
        for peer in freq_peers:
            send(
                term_last.at[peer, place, :], got_last.at[freq, place, :],
                last_send, last_recv.at[piece_no], (shot, row, peer),
            )

    @pl.loop(0, late_count - 1)
    def _(c):
        last_rows(span(c, late_step), c)

    @pl.loop(0, tail_count)
    def _(c):
        last_rows(tail_span(c), late_count + c)

    got_last[freq] = term_last[freq]
    other = pl.ds(pl.multiple_of((1 - chip) * half, half), half)
    wait_for(image.at[0, :, other], cross_recv.at[1 - chip])

    @pl.when(active)
    def _():
        wait_for(part_first.at[pl.ds(0, 3)], cross_send)

    @pl.when(jnp.logical_not(active))
    def _():
        wait_for(image.at[0, :, strip], cross_recv.at[chip])

    pltpu.make_async_copy(image.at[0], img_out.at[0], store_sem.at[2]).start()

    def last_sum(place, piece_no):
        wait_for(got_last.at[pl.ds(0, 3), place, :], last_recv.at[piece_no])
        image[1, place, :] = (got_last[0, place, :] + got_last[1, place, :]) + (
            got_last[2, place, :] + got_last[3, place, :]
        )

    @pl.loop(0, late_count - 1)
    def _(c):
        last_sum(span(c, late_step), c)

    @pl.loop(0, tail_count)
    def _(c):
        last_sum(tail_span(c), late_count + c)

    pltpu.make_async_copy(image.at[1], img_out.at[1], store_sem.at[3]).start()

    wait_for(piece.at[pl.ds(0, 3)], piece_send)
    for depth, ref in enumerate((grid_first, grid_last)):
        wait_for(masked.at[depth, pl.ds(0, 3)], shared_send.at[depth])
        wait_for(ref.at[0, pl.ds(0, 3)], depth_send.at[depth])
        wait_for(ref.at[0], across_send.at[depth])
    for which in range(2):
        wait_for(early.at[which, :, pl.ds(0, 3)], early_send.at[which])
        wait_for(store.at[which, pl.ds(0, 3)], late_send.at[which])
    for h in range(2):

        @pl.when(core + 2 * h != freq)
        def _(h=h):
            wait_for(term_first.at[h], first_send.at[h])

    wait_for(term_last.at[pl.ds(0, 3)], last_send)
    wait_for(field.at[0], store_sem.at[0])
    wait_for(field.at[1], store_sem.at[1])
    wait_for(image.at[0], store_sem.at[2])
    wait_for(image.at[1], store_sem.at[3])


def copy_kernel(count, *refs):
    places, outs, holds = refs[:count], refs[count : 2 * count], refs[2 * count : 3 * count]
    load_sem, store_sem = refs[3 * count :]
    loads = [pltpu.make_async_copy(places[i], holds[i], load_sem.at[i]) for i in range(count)]
    stores = [pltpu.make_async_copy(holds[i], outs[i], store_sem.at[i]) for i in range(count)]
    for load in loads:
        load.start()
    for load, store in zip(loads, stores):
        load.wait()
        store.start()
    for store in stores:
        store.wait()


def copied(arrays):
    any_spec = pl.BlockSpec(memory_space=pl.ANY)
    count = len(arrays)
    return pl.pallas_call(
        partial(copy_kernel, count),
        out_shape=[jax.ShapeDtypeStruct(a.shape, a.dtype) for a in arrays],
        in_specs=[any_spec] * count,
        out_specs=[any_spec] * count,
        scratch_shapes=[pltpu.VMEM(a.shape, a.dtype) for a in arrays] + [pltpu.SemaphoreType.DMA((count,))] * 2,
        compiler_params=pltpu.CompilerParams(vmem_limit_bytes=fused_vmem),
    )(*arrays)


def fused_body(table, source_field, receiver_field, slowness, owner, freq_index):
    rows, width = source_field.shape[2:]
    quarter = width // 4
    chunks = 8
    step = rows // chunks
    late_step = rows // 4
    tail_step = late_step // 2

    def floats(*shape):
        return pltpu.VMEM(shape, jnp.float32)

    dma = pltpu.SemaphoreType.DMA
    block = (4, 2, rows, quarter)
    small = pl.BlockSpec(memory_space=pltpu.SMEM)
    any_spec = pl.BlockSpec(memory_space=pl.ANY)
    outs = pl.pallas_call(
        partial(fused_kernel, step, late_step, tail_step),
        out_shape=[
            jax.ShapeDtypeStruct(source_field.shape, jnp.float32),
            jax.ShapeDtypeStruct(source_field.shape, jnp.float32),
            jax.ShapeDtypeStruct((2, rows, quarter), jnp.float32),
        ],
        in_specs=[small] * 2 + [any_spec] * 4,
        out_specs=[any_spec] * 3,
        scratch_shapes=[
            floats(2, 2, rows, width),
            floats(*table.shape),
            pltpu.VMEM((8, 2 * quarter, 2 * quarter), jnp.bfloat16),
            floats(rows, width),
            floats(2, chunks, 4, 2, step, quarter),
            floats(2, *block),
            floats(*block),
            floats(4, *block),
            floats(2, 4, rows // 8, width),
            floats(2, 4, rows // 8, width),
            floats(4, rows // 8, quarter),
            floats(2, 4, 4, rows // 8, quarter),
            floats(2, 4, rows // 8, width),
            floats(4, rows, quarter),
            floats(4, rows, quarter),
            floats(rows, width),
            floats(rows, width),
            floats(2, 4, rows, quarter // 2),
            floats(4, 4, rows, quarter // 2),
            floats(4, rows, quarter // 2),
            floats(4, rows, quarter),
            floats(4, rows, quarter),
            floats(2, rows, quarter),
            dma((6,)), dma((4,)), dma((2,)), dma((2,)), dma((2, 2)), dma((2,)), dma((2, 16)),
            dma((2,)), dma((2,)), dma, dma, dma((2,)), dma((2, 4)), dma((2,)), dma((2,)),
            dma((2,)), dma((4,)), dma, dma((2,)), dma, dma((16,)),
        ],
        compiler_params=pltpu.CompilerParams(
            collective_id=0, has_side_effects=True, vmem_limit_bytes=fused_vmem
        ),
    )(owner, freq_index, source_field, receiver_field, slowness, table)
    return tuple(copied(outs))


def solution(mesh):
    in_specs = (
        P(None, ("shot", "freq"), "row", None),
        P(None, ("shot", "freq"), "row", None),
        P("freq", "row", None),
        P(),
        P(("shot", "freq")),
    )
    out_specs = (
        P(None, ("shot", "freq"), "row", None),
        P(None, ("shot", "freq"), "row", None),
        P("shot", "row", "freq"),
    )
    sizes = tuple(mesh.shape[name] for name in ("shot", "row", "freq"))

    def whole_program(source_field, *rest):
        height, width = source_field.shape[2:]
        part = body
        if sizes == (2, 4, 4) and height == width and width % 1024 == 0:
            part = partial(fused_body, filter_table(width, sizes[2]))
        return jax.shard_map(part, mesh=mesh, in_specs=in_specs, out_specs=out_specs, check_vma=False)(
            source_field, *rest
        )

    return whole_program
```
